128 devices in a mesh: px: 8 (over x, core), py: 16 (over y, z).
Axes of the slice: x: 4, y: 4, z: 4, core: 2. Of those that a mesh axis runs over, the one named last changes fastest.
Arguments:
- root_density: float32 [384, 384, 384], P('px', 'py'), may hold values from -6 to 6
- subgrid_density: float32 [2048, 32, 1024], P(('px', 'py')), may hold values from -24 to 24
- velocity: float32 [3, 2048, 32, 1024], P(None, ('px', 'py')), may hold values from -6 to 6
- slot_anchor: int32 [3, 2048], replicated, may hold values from 0 to 376, as said below
- slot_count: int32 [128], replicated, may hold values from 1 to 16, as said below
- neighbour: int32 [2, 2048], replicated, may hold values from -1 to 2047, as said below
Outputs:
- coarse_potential: float32 [384, 384, 384], P('px', 'py')
- subgrid_potential: float32 [2048, 32, 1024], P(('px', 'py'))
- kicked_velocity: float32 [3, 2048, 32, 1024], P(None, ('px', 'py'))
The draws below stay inside these ranges and needn't reach their ends.
Inputs may be any that keep to these rules, and one draw needn't show every extreme that they name: Slot j of device d is slot d * 16 + j, devices numbered in the order of px+py; it is live when j < slot_count[d]. Some device has every slot live. `slot_anchor`: entries are multiples of 8; live slots cover distinct regions of 8^3 root cells; empty slots hold 0. The region of live slot j of the device at px = p, py = q has its lower corner among the root cells that the device at px = p, py = (q + j) mod 16 holds of root_density. neighbour[0, s] is s - 16 or -1 and neighbour[1, s] is s + 16 or -1, the same slot of the device one index lower or higher along py with the same px; where set, both slots are live and the two regions lie next to each other along the second dimension, the lower one below. Empty slots hold -1.
All inputs are finite; a program needn't handle non-finite values.
Results may differ from the reference program's by a relative error of at most 0.000094.
Values sent between devices are 32-bit elements; how exact they have to be, the bound alone decides.
No kernel may reach another device: no remote copies, remote signals or barrier semaphores. Data moves between devices by JAX's collectives and lax.ppermute only.
A program may use at most 128 MiB of HBM per device.

```python
import jax
import jax.numpy as jnp
from jax import lax

NR = 384
REG = 8
REF = 4
SWEEPS = 4
SUBGRID_CELLS = 32
DEVICE_SLOTS = 16
TOTAL_SLOTS = 2048
DEVICES = 128


def slot_layout(key):
    base_key = jax.random.fold_in(key, 4021)
    count_key, busy_key, place_key, shift_random_key, border_key, face_side_key = jax.random.split(base_key, 6)
    rows_px = DEVICES // DEVICE_SLOTS
    wave_band = NR // DEVICE_SLOTS // REG
    first_band = NR // rows_px // REG
    third_band = NR // REG
    counts = jax.random.randint(count_key, (DEVICES,), 1, DEVICE_SLOTS + 1, dtype=jnp.int32)
    busiest = jax.random.permutation(busy_key, DEVICES)[:2]
    counts = counts.at[busiest].set(DEVICE_SLOTS)
    row_keys = jax.random.split(place_key, rows_px)
    picks = jax.vmap(lambda row_key: jax.random.permutation(row_key, first_band * third_band)[:DEVICE_SLOTS])(row_keys)
    picks = picks.astype(jnp.int32)
    slot_numbers = jnp.arange(TOTAL_SLOTS, dtype=jnp.int32)
    owners = slot_numbers // DEVICE_SLOTS
    within = slot_numbers % DEVICE_SLOTS
    row_place = owners // DEVICE_SLOTS
    column_place = owners % DEVICE_SLOTS
    live_mask = within < counts[owners]
    pair = picks[row_place, within]
    first = row_place * first_band + pair // third_band
    third = pair % third_band
    source_column = (column_place + within) % DEVICE_SLOTS
    constant_shift = jax.random.randint(shift_random_key, (TOTAL_SLOTS,), 0, wave_band, dtype=jnp.int32)
    border_face = jax.random.randint(border_key, (TOTAL_SLOTS,), 0, 2, dtype=jnp.int32)
    face_side = jax.random.randint(face_side_key, (TOTAL_SLOTS,), 0, 2, dtype=jnp.int32)
    offset = jnp.where(border_face == 1, face_side * (wave_band - 1), constant_shift)
    second = source_column * wave_band + offset
    anchor = jnp.stack([first * REG, second * REG, third * REG]).astype(jnp.int32)
    anchor = jnp.where(live_mask[None, :], anchor, 0)
    upper_neighbour_slot = jnp.minimum(slot_numbers + DEVICE_SLOTS, TOTAL_SLOTS - 1)
    has_upper = live_mask & (column_place < DEVICE_SLOTS - 1) & live_mask[upper_neighbour_slot] & (offset == wave_band - 1) & (offset[upper_neighbour_slot] == 0) & (source_column < DEVICE_SLOTS - 1)
    lower_id = jnp.maximum(slot_numbers - DEVICE_SLOTS, 0)
    has_lower = live_mask & (column_place > 0) & live_mask[lower_id] & (offset[lower_id] == wave_band - 1) & (offset == 0) & (source_column[lower_id] < DEVICE_SLOTS - 1)
    upper_slot = jnp.where(has_upper, slot_numbers + DEVICE_SLOTS, -1)
    lower_slot = jnp.where(has_lower, slot_numbers - DEVICE_SLOTS, -1)
    return (anchor, counts.astype(jnp.int32), jnp.stack([lower_slot, upper_slot]).astype(jnp.int32))


def draw_slot_anchor(key, part):
    return slot_layout(key)[0]


def draw_slot_count(key, part):
    return slot_layout(key)[1]


def draw_neighbour(key, part):
    return slot_layout(key)[2]


def draw_root_density(key, part):
    density = jnp.clip(jax.random.normal(jax.random.fold_in(key, 77), (NR, NR, NR), jnp.float32), -6.0, 6.0)
    return density


def steps_of(stream_key, shape, shards, least, high):
    gain = 1.0
    for position, parts in shards:
        steps = jax.random.uniform(jax.random.fold_in(jax.random.fold_in(stream_key, 6), position), (parts,), jnp.float32, least / len(shards), high / len(shards))
        gain = gain * jnp.repeat(jnp.exp(steps), shape[position] // parts).reshape((-1,) + (1,) * (len(shape) - 1 - position))
    return gain


def noise(own_key, extent, spread, most, cuts=(), kind=jnp.bfloat16):
    entries = spread * jax.random.normal(own_key, extent, jnp.float32)
    if cuts:
        entries = entries * steps_of(own_key, extent, cuts, -0.22, 0.18)
    return jnp.clip(entries, -most, most).astype(kind)


def setup_inputs(seed: int = 0) -> dict:
    key_of = jax.random.split(jax.random.key(seed), 7)
    root_density = draw_root_density(jax.random.fold_in(key_of[6], 71), 0)
    subgrid_density = noise(key_of[1], (TOTAL_SLOTS, SUBGRID_CELLS, SUBGRID_CELLS * SUBGRID_CELLS), 4.0, 24.0, ((0, 128),), jnp.float32)
    velocity = noise(key_of[2], (3, TOTAL_SLOTS, SUBGRID_CELLS, SUBGRID_CELLS * SUBGRID_CELLS), 1.0, 6.0, ((1, 128),), jnp.float32)
    slot_anchor = draw_slot_anchor(jax.random.fold_in(key_of[6], 71), 0)
    slot_count = draw_slot_count(jax.random.fold_in(key_of[6], 71), 0)
    neighbour = draw_neighbour(jax.random.fold_in(key_of[6], 71), 0)
    return {"root_density": root_density, "subgrid_density": subgrid_density, "velocity": velocity, "slot_anchor": slot_anchor, "slot_count": slot_count, "neighbour": neighbour}


HIGHEST_PRECISION = lax.Precision.HIGHEST
RELAXATION = 6.0 / 7.0


def eigenvalue(wavenumber):
    return -4.0 * jnp.sin((jnp.pi / NR) * wavenumber.astype(jnp.float32)) ** 2


def green_block(wave_first, wave_second, wave_third):
    total = eigenvalue(wave_first)[:, None, None] + eigenvalue(wave_second)[None, :, None] + eigenvalue(wave_third)[None, None, :]
    zero_mode = (wave_first[:, None, None] == 0) & (wave_second[None, :, None] == 0) & (wave_third[None, None, :] == 0)
    safe_total = jnp.where(zero_mode, -1.0, total)
    return jnp.where(zero_mode, 0.0, 1.0 / safe_total)


def weights_table():
    cells = jnp.arange(REG * REF + 2, dtype=jnp.int32)
    marks = 2 * cells - 1 + REF
    lower_cell = jnp.minimum(marks // (2 * REF), REG)
    fraction = (marks - 2 * REF * lower_cell).astype(jnp.float32) / (2 * REF)
    columns = jnp.arange(REG + 2, dtype=jnp.int32)
    return (jnp.where(columns[None, :] == lower_cell[:, None], 1.0 - fraction[:, None], 0.0)
            + jnp.where(columns[None, :] == lower_cell[:, None] + 1, fraction[:, None], 0.0))


def interpolate(patch, matrix):
    step_one = jnp.einsum("sabc,kc->sabk", patch, matrix, precision=HIGHEST_PRECISION)
    step_two = jnp.einsum("sabk,jb->sajk", step_one, matrix, precision=HIGHEST_PRECISION)
    return jnp.einsum("sajk,ia->sijk", step_two, matrix, precision=HIGHEST_PRECISION)


def extend(coarse, interior, below_face, above_face, use_below, use_above):
    grown = coarse.at[:, 1:-1, 1:-1, 1:-1].set(interior)
    grown = grown.at[:, 1:-1, 0, 1:-1].set(jnp.where(use_below[:, None, None], below_face, grown[:, 1:-1, 0, 1:-1]))
    grown = grown.at[:, 1:-1, -1, 1:-1].set(jnp.where(use_above[:, None, None], above_face, grown[:, 1:-1, -1, 1:-1]))
    return grown


def relax(grown, interior, density):
    beside_all = (grown[:, 2:, 1:-1, 1:-1] + grown[:, :-2, 1:-1, 1:-1]
              + grown[:, 1:-1, 2:, 1:-1] + grown[:, 1:-1, :-2, 1:-1]
              + grown[:, 1:-1, 1:-1, 2:] + grown[:, 1:-1, 1:-1, :-2])
    return (1.0 - RELAXATION) * interior + RELAXATION * (beside_all - density * (1.0 / (REF * REF))) / 6.0


def kick(grown, velocity, live_mask):
    scale_factor = REF / 2.0
    slope_first = (grown[:, 2:, 1:-1, 1:-1] - grown[:, :-2, 1:-1, 1:-1]) * scale_factor
    slope_second = (grown[:, 1:-1, 2:, 1:-1] - grown[:, 1:-1, :-2, 1:-1]) * scale_factor
    slope_third = (grown[:, 1:-1, 1:-1, 2:] - grown[:, 1:-1, 1:-1, :-2]) * scale_factor
    velocity_after_kick = velocity - jnp.stack([slope_first, slope_second, slope_third])
    return jnp.where(live_mask[None, :, None, None, None], velocity_after_kick, 0.0)


def reference(root_density, subgrid_density, velocity, slot_anchor, slot_count, neighbour):
    subgrid_cells = subgrid_density.reshape(TOTAL_SLOTS, SUBGRID_CELLS, SUBGRID_CELLS, SUBGRID_CELLS)
    cell_velocity = velocity.reshape(3, TOTAL_SLOTS, SUBGRID_CELLS, SUBGRID_CELLS, SUBGRID_CELLS)
    every_wave = jnp.arange(NR, dtype=jnp.int32)
    factor = green_block(every_wave, every_wave, every_wave)
    coarse_potential = jnp.real(jnp.fft.ifftn(jnp.fft.fftn(root_density) * factor)).astype(jnp.float32)
    slot_numbers = jnp.arange(TOTAL_SLOTS, dtype=jnp.int32)
    live_mask = (slot_numbers % DEVICE_SLOTS) < slot_count[slot_numbers // DEVICE_SLOTS]
    offsets = jnp.arange(REG + 2, dtype=jnp.int32)
    index_first = (slot_anchor[0][:, None] - 1 + offsets[None, :]) % NR
    index_second = (slot_anchor[1][:, None] - 1 + offsets[None, :]) % NR
    index_third = (slot_anchor[2][:, None] - 1 + offsets[None, :]) % NR
    patch = coarse_potential[index_first[:, :, None, None], index_second[:, None, :, None], index_third[:, None, None, :]]
    coarse = interpolate(patch, weights_table())
    interior = coarse[:, 1:-1, 1:-1, 1:-1]
    below_slot = jnp.maximum(neighbour[0], 0)
    above_slot = jnp.maximum(neighbour[1], 0)
    grown = coarse
    for sweep_index in range(SWEEPS + 1):
        grown = extend(coarse, interior, interior[below_slot, :, -1, :], interior[above_slot, :, 0, :],
                       neighbour[0] >= 0, neighbour[1] >= 0)
        if sweep_index < SWEEPS:
            interior = relax(grown, interior, subgrid_cells)
    subgrid_potential = jnp.where(live_mask[:, None, None, None], interior, 0.0)
    velocity_after_kick = kick(grown, cell_velocity, live_mask)
    return (coarse_potential, subgrid_potential.reshape(TOTAL_SLOTS, SUBGRID_CELLS, SUBGRID_CELLS * SUBGRID_CELLS),
            velocity_after_kick.reshape(3, TOTAL_SLOTS, SUBGRID_CELLS, SUBGRID_CELLS * SUBGRID_CELLS))
```

```python
import numpy as np
import jax
import jax.numpy as jnp
from jax import lax
from jax.experimental import pallas as pl
from jax.experimental.pallas import tpu as pltpu
from jax.sharding import PartitionSpec as P

NR = 384
REG = 8
REF = 4
SWEEPS = 4
CELLS = REG * REF
PX = 8
PY = 16
DEV = PX * PY
MODES = NR // DEV
XB = NR // PX
YB = NR // PY
XE = XB + 2
YE = YB + 4
PLANE = 1408
EDGE = 4
LANES = (CELLS + 2 * EDGE) * CELLS
RELAX = 6.0 / 7.0
HIGH = lax.Precision.HIGH


def fourier_basis():
    n = np.arange(NR)
    k = np.concatenate([[0, NR // 2], np.repeat(np.arange(1, NR // 2), 2)])
    phase = 2.0 * np.pi * ((n[:, None] * k[None, :]) % NR) / NR
    odd = np.zeros(NR, bool)
    odd[3::2] = True
    q = np.where(odd[None, :], np.sin(phase), np.cos(phase)) * np.sqrt(2.0 / NR)
    q[:, :2] *= np.sqrt(0.5)
    eig = -4.0 * np.sin(np.pi * k / NR) ** 2
    return q, eig


def line_weights(first, last, offset):
    cells = np.arange(first, last)
    marks = 2 * cells + 1 - REF
    low = marks // (2 * REF)
    frac = (marks - 2 * REF * low) / (2.0 * REF)
    table = np.zeros((len(cells), 16))
    rows = np.arange(len(cells))
    table[rows, low + offset] += 1.0 - frac
    table[rows, low + 1 + offset] += frac
    return table


def interpolation_tables():
    wi = line_weights(0, CELLS, 1)[:, :10]
    wlow = line_weights(-1, 0, 1)[:, :10]
    whigh = line_weights(CELLS, CELLS + 1, 1)[:, :10]
    wj = line_weights(-EDGE, CELLS + EDGE, 2)[:, :12]
    jlow = line_weights(-EDGE - 1, -EDGE, 2)[0, :12]
    jhigh = line_weights(CELLS + EDGE, CELLS + EDGE + 1, 2)[0, :12]
    inner = np.einsum("jb,kc->bcjk", wj, wi)
    edge = np.zeros_like(inner)
    edge[:, :, :, 0] += np.einsum("jb,c->bcj", wj, wlow[0])
    edge[:, :, :, -1] += np.einsum("jb,c->bcj", wj, whigh[0])
    edge[:, :, 0, :] += np.einsum("b,kc->bck", jlow, wi)
    edge[:, :, -1, :] += np.einsum("b,kc->bck", jhigh, wi)
    cols = np.zeros((128, 2 * LANES))
    cols[:120, :LANES] = inner.reshape(120, LANES)
    cols[:120, LANES:] = edge.reshape(120, LANES)
    rows = np.zeros((40, 16))
    rows[:32, :10] = wi
    rows[32, :10] = wlow[0]
    rows[33, :10] = whigh[0]
    return rows, cols


def from_behind(value, axis, steps):
    count = lax.axis_size(axis)
    initial, last = (max(0, -steps), min(count, count - steps))
    return lax.ppermute(value, axis, [(source, source + steps) for source in range(initial, last)])


def split3(x):
    hi = x.astype(jnp.bfloat16)
    rest = x - hi.astype(jnp.float32)
    mid = rest.astype(jnp.bfloat16)
    low = (rest - mid.astype(jnp.float32)).astype(jnp.bfloat16)
    return hi, mid, low


def dot(a, b):
    return jnp.dot(a, b, preferred_element_type=jnp.float32)


def cut_kernel(start_ref, s_ref, g_ref, out_ref, p_ref):
    cells = lax.dot_general(
        s_ref[...], g_ref[...], (((0,), (0,)), ((), ())),
        precision=lax.Precision.HIGHEST, preferred_element_type=jnp.float32)
    for y in range(YE):
        p_ref[y, :XE, :] = cells[y * XE:(y + 1) * XE, :]
    lane = lax.broadcasted_iota(jnp.int32, (16, 128), 1)
    for t in range(PY):
        acc = jnp.zeros((16, 128), jnp.float32)
        for b in range(12):
            first = pl.multiple_of(start_ref[0, t], 8)
            tile = p_ref[start_ref[1, t] + b, pl.ds(first, 16), (t // 8) * 128:(t // 8 + 1) * 128]
            shift = (b * 10 - (t % 8) * 16) % 128
            if shift:
                tile = pltpu.roll(tile, shift, 1)
            acc = jnp.where((lane >= b * 10) & (lane < b * 10 + 10), tile, acc)
        out_ref[t * 16:(t + 1) * 16, :] = acc


def cut_patches(spectrum, columns, starts):
    return pl.pallas_call(
        cut_kernel,
        out_shape=jax.ShapeDtypeStruct((PY * 16, 128), jnp.float32),
        in_specs=[pl.BlockSpec(memory_space=pltpu.SMEM),
                  pl.BlockSpec(memory_space=pltpu.VMEM),
                  pl.BlockSpec(memory_space=pltpu.VMEM)],
        out_specs=pl.BlockSpec(memory_space=pltpu.VMEM),
        scratch_shapes=[pltpu.VMEM((YE, 56, 256), jnp.float32)],
        compiler_params=pltpu.CompilerParams(vmem_limit_bytes=48 << 20),
        name="cut_patches",
    )(starts, spectrum, columns)


def relax_kernel(flag_ref, patch_ref, rows_ref, cols_ref, dens_ref, low_ref, high_ref, vel_ref,
                 pot_ref, out_ref, grid_ref):
    step = pl.program_id(0)

    @pl.when(step == 0)
    def _():
        rows = rows_ref[...]
        expanded = jnp.zeros((640, 128), jnp.float32)
        ordered = jnp.concatenate(
            [patch_ref[pl.ds(pl.multiple_of(flag_ref[j, 5] * 16, 16), 16), :] for j in range(PY)], axis=0)
        for part in split3(ordered):
            expanded += dot(rows, part)
        parts = split3(expanded)
        for n in range(0, 2 * LANES, 256):
            table = cols_ref[:, n:n + 256]
            acc = dot(parts[0], table) + dot(parts[1], table) + dot(parts[2], table)
            grid_ref[:, n:n + 256] = acc

    base = pl.multiple_of(step * 40, 8)
    v0 = grid_ref[pl.ds(base, 32), :LANES]
    edge = grid_ref[pl.ds(base, 32), LANES:]
    faces = grid_ref[pl.ds(base + 32, 8), :LANES]
    lane = lax.broadcasted_iota(jnp.int32, (32, LANES), 1)
    row = lax.broadcasted_iota(jnp.int32, (32, LANES), 0)
    third = lane % CELLS
    low_face = jnp.broadcast_to(faces[0:1], (32, LANES))
    high_face = jnp.broadcast_to(faces[1:2], (32, LANES))
    first_row = row == 0
    last_row = row == CELLS - 1
    zero = jnp.zeros((32, LANES), jnp.float32)
    density = jnp.concatenate([low_ref[0], dens_ref[0], high_ref[0]], axis=1)
    fixed = edge + jnp.where(first_row, low_face, zero) + jnp.where(last_row, high_face, zero)
    c = RELAX / 6.0
    fixed = c * (fixed - density * (1.0 / (REF * REF)))
    use_low = flag_ref[step, 0] > 0
    use_high = flag_ref[step, 1] > 0
    same_low = flag_ref[step, 2] > 0
    same_high = flag_ref[step, 3] > 0
    live = flag_ref[step, 4] > 0
    in_low = lane < EDGE * CELLS
    in_high = lane >= (EDGE + CELLS) * CELLS
    held = (in_low & jnp.logical_not(use_low)) | (in_high & jnp.logical_not(use_high))
    frozen_next = (lane >= (EDGE - 1) * CELLS) & in_low & jnp.logical_not(same_low)
    frozen_prev = in_high & (lane < (EDGE + CELLS + 1) * CELLS) & jnp.logical_not(same_high)

    def beside(v):
        prev_third = jnp.where(third == 0, zero, pltpu.roll(v, 1, 1))
        next_third = jnp.where(third == CELLS - 1, zero, pltpu.roll(v, LANES - 1, 1))
        prev_first = jnp.where(first_row, zero, pltpu.roll(v, 1, 0))
        next_first = jnp.where(last_row, zero, pltpu.roll(v, CELLS - 1, 0))
        prev_second = pltpu.roll(v, CELLS, 1)
        next_second = pltpu.roll(v, LANES - CELLS, 1)
        return prev_first, next_first, prev_second, next_second, prev_third, next_third

    start_prev = pltpu.roll(v0, CELLS, 1)
    start_next = pltpu.roll(v0, LANES - CELLS, 1)
    outer_low = lane < CELLS
    outer_high = lane >= LANES - CELLS
    v = v0
    for _ in range(SWEEPS):
        pf, nf, ps, ns, pt, nt = beside(v)
        ps = jnp.where(outer_low, zero, jnp.where(frozen_prev, start_prev, ps))
        ns = jnp.where(outer_high, zero, jnp.where(frozen_next, start_next, ns))
        new = (1.0 - RELAX) * v + c * (pf + nf + ps + ns + pt + nt) + fixed
        v = jnp.where(held, v, new)
    pf, nf, ps, ns, pt, nt = beside(v)
    own = slice(EDGE * CELLS, (EDGE + CELLS) * CELLS)
    scale = REF / 2.0
    slope_first = (nf + jnp.where(last_row, high_face, zero)) - (pf + jnp.where(first_row, low_face, zero))
    slope_second = ns - ps
    slope_third = (nt + jnp.where(third == CELLS - 1, edge, zero)) - (pt + jnp.where(third == 0, edge, zero))
    pot_ref[0] = jnp.where(live, v[:, own], 0.0)
    for q, slope in enumerate((slope_first, slope_second, slope_third)):
        out_ref[q, 0] = jnp.where(live, vel_ref[q, 0] - slope[:, own] * scale, 0.0)


def relax(flags, patch, density, low, high, velocity):
    slots = density.shape[0]
    rows, cols = interpolation_tables()
    block_rows = jnp.asarray(np.kron(np.eye(slots), rows), jnp.bfloat16)
    table = jnp.asarray(cols, jnp.bfloat16)
    whole = lambda shape: pl.BlockSpec(shape, lambda s, f: (0,) * len(shape), pipeline_mode=pl.Buffered(1))
    return pl.pallas_call(
        relax_kernel,
        grid_spec=pltpu.PrefetchScalarGridSpec(
            num_scalar_prefetch=1,
            grid=(slots,),
            in_specs=[
                whole((slots * 16, 128)),
                whole((slots * 40, slots * 16)),
                whole((128, 2 * LANES)),
                pl.BlockSpec((1, CELLS, CELLS * CELLS), lambda s, f: (s, 0, 0)),
                pl.BlockSpec((1, CELLS, EDGE * CELLS), lambda s, f: (s, 0, 0)),
                pl.BlockSpec((1, CELLS, EDGE * CELLS), lambda s, f: (s, 0, 0)),
                pl.BlockSpec((3, 1, CELLS, CELLS * CELLS), lambda s, f: (0, s, 0, 0)),
            ],
            out_specs=[
                pl.BlockSpec((1, CELLS, CELLS * CELLS), lambda s, f: (s, 0, 0)),
                pl.BlockSpec((3, 1, CELLS, CELLS * CELLS), lambda s, f: (0, s, 0, 0)),
            ],
            scratch_shapes=[pltpu.VMEM((slots * 40, 2 * LANES), jnp.float32)],
        ),
        out_shape=[
            jax.ShapeDtypeStruct(density.shape, jnp.float32),
            jax.ShapeDtypeStruct(velocity.shape, jnp.float32),
        ],
        compiler_params=pltpu.CompilerParams(vmem_limit_bytes=48 << 20),
        name="relax_and_kick",
    )(flags, patch, block_rows, table, density, low, high, velocity)


def local(root_density, subgrid_density, velocity, slot_anchor, slot_count, neighbour):
    place_first = lax.axis_index("px")
    place_second = lax.axis_index("py")
    device = place_first * PY + place_second
    slots = subgrid_density.shape[0]
    q, eig = fourier_basis()
    basis = jnp.asarray(q, jnp.float32)
    eigen = jnp.asarray(eig, jnp.float32)
    low = from_behind(subgrid_density[:, :, -EDGE * CELLS:], "py", 1)
    high = from_behind(subgrid_density[:, :, :EDGE * CELLS], "py", -1)

    packed = jnp.einsum("xyz,zmt->tmyx", root_density, basis.reshape(NR, MODES, DEV), precision=HIGH)
    got = lax.all_to_all(packed.reshape(DEV, MODES * YB * XB), ("px", "py"), 0, 0, tiled=True)
    planes = got.reshape(PX, PY, MODES, YB, XB).transpose(2, 3, 1, 0, 4).reshape(MODES, NR, NR)
    n = np.arange(NR)
    order = (n % PY) * YB + n // PY
    wide = ((np.arange(YE)[:, None] - 2 + np.arange(PY)[None, :] * YB) % NR).reshape(-1)
    wide_x = ((np.arange(PX)[:, None] * XB + np.arange(XE)[None, :] - 1) % NR).reshape(-1)
    z = jnp.einsum("myx,xk->myk", planes, basis, precision=HIGH)
    z = jnp.einsum("myk,yl->mlk", z, jnp.asarray(q[order], jnp.float32), precision=HIGH)
    own_eig = eigen[jnp.arange(MODES) * DEV + device]
    total = own_eig[:, None, None] + eigen[None, :, None] + eigen[None, None, :]
    is_zero = total == 0.0
    z = z * jnp.where(is_zero, 0.0, 1.0 / jnp.where(is_zero, -1.0, total))
    z = jnp.einsum("mlk,yl->myk", z, jnp.asarray(q[wide], jnp.float32), precision=HIGH)
    z = jnp.einsum("myk,xk->myx", z, jnp.asarray(q[wide_x], jnp.float32), precision=HIGH)
    z = z.reshape(MODES, YE, PY, PX, XE).transpose(3, 2, 0, 1, 4).reshape(DEV, MODES, YE * XE)
    z = jnp.pad(z, ((0, 0), (0, 0), (0, PLANE - YE * XE))).reshape(DEV, MODES * PLANE)
    back = lax.all_to_all(z, ("px", "py"), 0, 0, tiled=True)
    spectrum = back.reshape(DEV, MODES, PLANE).transpose(1, 0, 2).reshape(NR, PLANE)

    targets = jnp.arange(PY, dtype=jnp.int32)
    wanted = (place_first * PY + targets) * slots + (place_second - targets) % PY
    anchors = slot_anchor[:, wanted]
    third = (anchors[2][:, None] - 1 + jnp.arange(16, dtype=jnp.int32)[None, :]) % NR
    columns = basis[third.reshape(-1)].T
    start_first = jnp.clip(anchors[0] - place_first * XB, 0, XB - REG)
    start_second = jnp.clip(anchors[1] - place_second * YB, 0, YB - REG)
    sending = cut_patches(spectrum, columns, jnp.stack([start_first, start_second]))
    arrived = lax.all_to_all(sending, "py", 0, 0, tiled=True)
    positions = jnp.arange(slots, dtype=jnp.int32)

    block = jnp.einsum("nc,zn->cz", spectrum, basis, precision=HIGH)
    block = block[:YE * XE].reshape(YE, XE, NR)[2:-2, 1:-1]
    coarse_potential = block.transpose(1, 0, 2)

    first_slot = device * slots
    padded = jnp.pad(neighbour, ((0, 0), (slots, slots)), constant_values=-1)
    nearby = lax.dynamic_slice_in_dim(neighbour, first_slot, slots, 1)
    below = lax.dynamic_slice_in_dim(padded, first_slot, slots, 1)
    above = lax.dynamic_slice_in_dim(padded, first_slot + 2 * slots, slots, 1)
    flags = jnp.stack([
        nearby[0] >= 0, nearby[1] >= 0, below[1] >= 0, above[0] >= 0,
        positions < slot_count[device], (place_second + positions) % PY,
    ], axis=1).astype(jnp.int32)
    subgrid_potential, kicked = relax(flags, arrived, subgrid_density, low, high, velocity)
    return coarse_potential, subgrid_potential, kicked


def solution(mesh):
    return jax.shard_map(
        local,
        mesh=mesh,
        in_specs=(
            P("px", "py", None),
            P(("px", "py"), None, None),
            P(None, ("px", "py"), None, None),
            P(),
            P(),
            P(),
        ),
        out_specs=(
            P("px", "py", None),
            P(("px", "py"), None, None),
            P(None, ("px", "py"), None, None),
        ),
        check_vma=False,
    )
```

```python
import ml_dtypes
import numpy as np
import jax
import jax.numpy as jnp
from jax import lax
from jax.experimental import pallas as pl
from jax.experimental.pallas import tpu as pltpu
from jax.sharding import PartitionSpec as P

NR = 384
REG = 8
REF = 4
SWEEPS = 4
CELLS = REG * REF
PX = 8
PY = 16
DEV = PX * PY
MODES = NR // DEV
XB = NR // PX
YB = NR // PY
XE = XB + 2
YE = YB + 4
PLANE = 1408
EDGE = 4
LANES = (CELLS + 2 * EDGE) * CELLS
RELAX = 6.0 / 7.0
HIGH = lax.Precision.HIGH


def fourier_basis():
    n = np.arange(NR)
    k = np.concatenate([[0, NR // 2], np.repeat(np.arange(1, NR // 2), 2)])
    phase = 2.0 * np.pi * ((n[:, None] * k[None, :]) % NR) / NR
    odd = np.zeros(NR, bool)
    odd[3::2] = True
    q = np.where(odd[None, :], np.sin(phase), np.cos(phase)) * np.sqrt(2.0 / NR)
    q[:, :2] *= np.sqrt(0.5)
    eig = -4.0 * np.sin(np.pi * k / NR) ** 2
    return q, eig


def line_weights(first, last, offset):
    cells = np.arange(first, last)
    marks = 2 * cells + 1 - REF
    low = marks // (2 * REF)
    frac = (marks - 2 * REF * low) / (2.0 * REF)
    table = np.zeros((len(cells), 16))
    rows = np.arange(len(cells))
    table[rows, low + offset] += 1.0 - frac
    table[rows, low + 1 + offset] += frac
    return table


def interpolation_tables():
    wi = line_weights(0, CELLS, 1)[:, :10]
    wlow = line_weights(-1, 0, 1)[:, :10]
    whigh = line_weights(CELLS, CELLS + 1, 1)[:, :10]
    wj = line_weights(-EDGE, CELLS + EDGE, 2)[:, :12]
    jlow = line_weights(-EDGE - 1, -EDGE, 2)[0, :12]
    jhigh = line_weights(CELLS + EDGE, CELLS + EDGE + 1, 2)[0, :12]
    inner = np.einsum("jb,kc->bcjk", wj, wi)
    edge = np.zeros_like(inner)
    edge[:, :, :, 0] += np.einsum("jb,c->bcj", wj, wlow[0])
    edge[:, :, :, -1] += np.einsum("jb,c->bcj", wj, whigh[0])
    edge[:, :, 0, :] += np.einsum("b,kc->bck", jlow, wi)
    edge[:, :, -1, :] += np.einsum("b,kc->bck", jhigh, wi)
    cols = np.zeros((128, 2 * LANES))
    cols[:120, :LANES] = inner.reshape(120, LANES)
    cols[:120, LANES:] = edge.reshape(120, LANES)
    rows = np.zeros((40, 16))
    rows[:32, :10] = wi
    rows[32, :10] = wlow[0]
    rows[33, :10] = whigh[0]
    return rows, cols


def from_behind(value, axis, steps):
    count = lax.axis_size(axis)
    initial, last = (max(0, -steps), min(count, count - steps))
    return lax.ppermute(value, axis, [(source, source + steps) for source in range(initial, last)])


def split3(x):
    hi = x.astype(jnp.bfloat16)
    rest = x - hi.astype(jnp.float32)
    mid = rest.astype(jnp.bfloat16)
    low = (rest - mid.astype(jnp.float32)).astype(jnp.bfloat16)
    return hi, mid, low


def dot(a, b):
    return jnp.dot(a, b, preferred_element_type=jnp.float32)


def split2(x):
    hi = x.astype(jnp.bfloat16)
    return hi, (x - hi.astype(jnp.float32)).astype(jnp.bfloat16)


def table_pair(table):
    hi = np.asarray(table, np.float32).astype(ml_dtypes.bfloat16)
    low = (np.asarray(table) - hi.astype(np.float64)).astype(ml_dtypes.bfloat16)
    return jnp.asarray(np.stack([hi, low]))


def right_product(x, pair):
    hi, low = split2(x)
    return dot(hi, pair[0]) + dot(low, pair[0]) + dot(hi, pair[1])


def left_product(pair, x):
    hi, low = split2(x)
    return dot(pair[0], hi) + dot(pair[0], low) + dot(pair[1], hi)


def moved(tiles, source, target, width, lane, out):
    shift = (target - source) % 128
    rolled = {}
    begin = 0
    while begin < width:
        src, dst = source + begin, target + begin
        end = min(width, begin + 128 - src % 128, begin + 128 - dst % 128)
        if src // 128 not in rolled:
            tile = tiles(src // 128)
            rolled[src // 128] = pltpu.roll(tile, shift, 1) if shift else tile
        tile = rolled[src // 128]
        first, last = dst % 128, dst % 128 + end - begin
        old = out[dst // 128]
        if old is None or first == 0:
            out[dst // 128] = tile
        else:
            out[dst // 128] = jnp.where(lane >= first, tile, old)
        begin = end


def plane_kernel(mode_ref, in_ref, ax_ref, ay_ref, by_ref, bx_ref, ey_ref, ex_ref, out_ref, x_ref, o_ref):
    lane = lax.broadcasted_iota(jnp.int32, (PY, 128), 1)
    for y in range(YB):
        out = [None] * 3
        for p in range(PX):
            rows = slice(p * PY, (p + 1) * PY)
            moved(lambda t: in_ref[rows, t * 128:(t + 1) * 128], y * XB, p * XB, XB, lane, out)
        for t in range(3):
            x_ref[y * PY:(y + 1) * PY, t * 128:(t + 1) * 128] = out[t]
    z = right_product(x_ref[...], ax_ref)
    z = left_product(ay_ref, z)
    total = mode_ref[pl.program_id(0)] + ey_ref[...] + ex_ref[...]
    is_zero = total == 0.0
    z = jnp.where(is_zero, 0.0, z / jnp.where(is_zero, -1.0, total))
    z = left_product(by_ref, z)
    o_ref[...] = right_product(z, bx_ref)
    for p in range(PX):
        out = [None] * (PLANE // 128)
        for y in range(YE):
            rows = slice(y * PY, (y + 1) * PY)
            moved(lambda t: o_ref[rows, t * 128:(t + 1) * 128], p * 64, y * XE, XE, lane, out)
        for t in range(PLANE // 128):
            out_ref[p * PY:(p + 1) * PY, t * 128:(t + 1) * 128] = out[t]


def solve_planes(own_eig, got, q, eig):
    n = np.arange(NR)
    order = (n % PY) * YB + n // PY
    wide = ((np.arange(YE)[:, None] - 2 + np.arange(PY)[None, :] * YB) % NR).reshape(-1)
    wide_x = np.zeros((PX, 64, NR))
    for p in range(PX):
        wide_x[p, :XE] = q[(p * XB + np.arange(XE) - 1) % NR]
    tables = [q, q[order].T, q[wide], wide_x.reshape(PX * 64, NR).T]
    tables = [table_pair(table) for table in tables]
    ey = jnp.asarray(eig[:, None], jnp.float32)
    ex = jnp.asarray(eig[None, :], jnp.float32)
    whole = lambda shape: pl.BlockSpec(shape, lambda m: (0,) * len(shape), pipeline_mode=pl.Buffered(1))
    return pl.pallas_call(
        plane_kernel,
        grid=(MODES,),
        out_shape=jax.ShapeDtypeStruct((DEV, MODES * PLANE), jnp.float32),
        in_specs=[pl.BlockSpec(memory_space=pltpu.SMEM),
                  pl.BlockSpec((DEV, XB * YB), lambda m: (0, m))]
        + [whole(table.shape) for table in tables] + [whole(ey.shape), whole(ex.shape)],
        out_specs=pl.BlockSpec((DEV, PLANE), lambda m: (0, m)),
        scratch_shapes=[pltpu.VMEM((NR, NR), jnp.float32), pltpu.VMEM((YE * PY, PX * 64), jnp.float32)],
        compiler_params=pltpu.CompilerParams(vmem_limit_bytes=48 << 20),
        name="solve_planes",
    )(own_eig, got, *tables, ey, ex)


def columns_of(s_ref, pair):
    total = None
    for m in range(MODES):
        hi, low = split2(s_ref[:, m * PLANE:(m + 1) * PLANE])
        rows = slice(m * DEV, (m + 1) * DEV)
        for left, right in ((hi, pair[0, rows]), (low, pair[0, rows]), (hi, pair[1, rows])):
            part = lax.dot_general(left, right, (((0,), (0,)), ((), ())), preferred_element_type=jnp.float32)
            total = part if total is None else total + part
    return total


def cut_kernel(start_ref, s_ref, g_ref, out_ref, p_ref):
    cells = columns_of(s_ref, jnp.stack(split2(g_ref[...])))
    for y in range(YE):
        p_ref[y, :XE, :] = cells[y * XE:(y + 1) * XE, :]
    lane = lax.broadcasted_iota(jnp.int32, (16, 128), 1)
    for t in range(PY):
        acc = jnp.zeros((16, 128), jnp.float32)
        for b in range(12):
            first = pl.multiple_of(start_ref[0, t], 8)
            tile = p_ref[start_ref[1, t] + b, pl.ds(first, 16), (t // 8) * 128:(t // 8 + 1) * 128]
            shift = (b * 10 - (t % 8) * 16) % 128
            if shift:
                tile = pltpu.roll(tile, shift, 1)
            acc = jnp.where((lane >= b * 10) & (lane < b * 10 + 10), tile, acc)
        out_ref[t * 16:(t + 1) * 16, :] = acc


def cut_patches(spectrum, columns, starts):
    return pl.pallas_call(
        cut_kernel,
        out_shape=jax.ShapeDtypeStruct((PY * 16, 128), jnp.float32),
        in_specs=[pl.BlockSpec(memory_space=pltpu.SMEM),
                  pl.BlockSpec(memory_space=pltpu.VMEM),
                  pl.BlockSpec(memory_space=pltpu.VMEM)],
        out_specs=pl.BlockSpec(memory_space=pltpu.VMEM),
        scratch_shapes=[pltpu.VMEM((YE, 56, 256), jnp.float32)],
        compiler_params=pltpu.CompilerParams(vmem_limit_bytes=48 << 20),
        name="cut_patches",
    )(starts, spectrum, columns)


def block_kernel(s_ref, q_ref, out_ref):
    cells = columns_of(s_ref, q_ref)
    for y in range(YB):
        first = (y + 2) * XE + 1
        out_ref[:, y, :] = cells[first:first + XB, :]


def block_of(spectrum, q):
    return pl.pallas_call(
        block_kernel,
        out_shape=jax.ShapeDtypeStruct((XB, YB, NR), jnp.float32),
        in_specs=[pl.BlockSpec(memory_space=pltpu.VMEM), pl.BlockSpec(memory_space=pltpu.VMEM)],
        out_specs=pl.BlockSpec(memory_space=pltpu.VMEM),
        compiler_params=pltpu.CompilerParams(vmem_limit_bytes=48 << 20),
        name="block_of",
    )(spectrum, table_pair(q.T))


def relax_kernel(flag_ref, patch_ref, rows_ref, cols_ref, dens_ref, low_ref, high_ref, vel_ref,
                 pot_ref, out_ref, grid_ref):
    step = pl.program_id(0)

    @pl.when(step == 0)
    def _():
        rows = rows_ref[...]
        expanded = jnp.zeros((640, 128), jnp.float32)
        ordered = jnp.concatenate(
            [patch_ref[pl.ds(pl.multiple_of(flag_ref[j, 5] * 16, 16), 16), :] for j in range(PY)], axis=0)
        for part in split3(ordered):
            expanded += dot(rows, part)
        parts = split3(expanded)
        for n in range(0, 2 * LANES, 256):
            table = cols_ref[:, n:n + 256]
            acc = dot(parts[0], table) + dot(parts[1], table) + dot(parts[2], table)
            grid_ref[:, n:n + 256] = acc

    base = pl.multiple_of(step * 40, 8)
    v0 = grid_ref[pl.ds(base, 32), :LANES]
    edge = grid_ref[pl.ds(base, 32), LANES:]
    faces = grid_ref[pl.ds(base + 32, 8), :LANES]
    lane = lax.broadcasted_iota(jnp.int32, (32, LANES), 1)
    row = lax.broadcasted_iota(jnp.int32, (32, LANES), 0)
    third = lane % CELLS
    low_face = jnp.broadcast_to(faces[0:1], (32, LANES))
    high_face = jnp.broadcast_to(faces[1:2], (32, LANES))
    first_row = row == 0
    last_row = row == CELLS - 1
    zero = jnp.zeros((32, LANES), jnp.float32)
    density = jnp.concatenate([low_ref[0], dens_ref[0], high_ref[0]], axis=1)
    fixed = edge + jnp.where(first_row, low_face, zero) + jnp.where(last_row, high_face, zero)
    c = RELAX / 6.0
    fixed = c * (fixed - density * (1.0 / (REF * REF)))
    use_low = flag_ref[step, 0] > 0
    use_high = flag_ref[step, 1] > 0
    same_low = flag_ref[step, 2] > 0
    same_high = flag_ref[step, 3] > 0
    live = flag_ref[step, 4] > 0
    in_low = lane < EDGE * CELLS
    in_high = lane >= (EDGE + CELLS) * CELLS
    held = (in_low & jnp.logical_not(use_low)) | (in_high & jnp.logical_not(use_high))
    frozen_next = (lane >= (EDGE - 1) * CELLS) & in_low & jnp.logical_not(same_low)
    frozen_prev = in_high & (lane < (EDGE + CELLS + 1) * CELLS) & jnp.logical_not(same_high)

    def beside(v):
        prev_third = jnp.where(third == 0, zero, pltpu.roll(v, 1, 1))
        next_third = jnp.where(third == CELLS - 1, zero, pltpu.roll(v, LANES - 1, 1))
        prev_first = jnp.where(first_row, zero, pltpu.roll(v, 1, 0))
        next_first = jnp.where(last_row, zero, pltpu.roll(v, CELLS - 1, 0))
        prev_second = pltpu.roll(v, CELLS, 1)
        next_second = pltpu.roll(v, LANES - CELLS, 1)
        return prev_first, next_first, prev_second, next_second, prev_third, next_third

    start_prev = pltpu.roll(v0, CELLS, 1)
    start_next = pltpu.roll(v0, LANES - CELLS, 1)
    outer_low = lane < CELLS
    outer_high = lane >= LANES - CELLS
    v = v0
    for _ in range(SWEEPS):
        pf, nf, ps, ns, pt, nt = beside(v)
        ps = jnp.where(outer_low, zero, jnp.where(frozen_prev, start_prev, ps))
        ns = jnp.where(outer_high, zero, jnp.where(frozen_next, start_next, ns))
        new = (1.0 - RELAX) * v + c * (pf + nf + ps + ns + pt + nt) + fixed
        v = jnp.where(held, v, new)
    pf, nf, ps, ns, pt, nt = beside(v)
    own = slice(EDGE * CELLS, (EDGE + CELLS) * CELLS)
    scale = REF / 2.0
    slope_first = (nf + jnp.where(last_row, high_face, zero)) - (pf + jnp.where(first_row, low_face, zero))
    slope_second = ns - ps
    slope_third = (nt + jnp.where(third == CELLS - 1, edge, zero)) - (pt + jnp.where(third == 0, edge, zero))
    pot_ref[0] = jnp.where(live, v[:, own], 0.0)
    for q, slope in enumerate((slope_first, slope_second, slope_third)):
        out_ref[q, 0] = jnp.where(live, vel_ref[q, 0] - slope[:, own] * scale, 0.0)


def relax(flags, patch, density, low, high, velocity):
    slots = density.shape[0]
    rows, cols = interpolation_tables()
    block_rows = jnp.asarray(np.kron(np.eye(slots), rows), jnp.bfloat16)
    table = jnp.asarray(cols, jnp.bfloat16)
    whole = lambda shape: pl.BlockSpec(shape, lambda s, f: (0,) * len(shape), pipeline_mode=pl.Buffered(1))
    return pl.pallas_call(
        relax_kernel,
        grid_spec=pltpu.PrefetchScalarGridSpec(
            num_scalar_prefetch=1,
            grid=(slots,),
            in_specs=[
                whole((slots * 16, 128)),
                whole((slots * 40, slots * 16)),
                whole((128, 2 * LANES)),
                pl.BlockSpec((1, CELLS, CELLS * CELLS), lambda s, f: (s, 0, 0)),
                pl.BlockSpec((1, CELLS, EDGE * CELLS), lambda s, f: (s, 0, 0)),
                pl.BlockSpec((1, CELLS, EDGE * CELLS), lambda s, f: (s, 0, 0)),
                pl.BlockSpec((3, 1, CELLS, CELLS * CELLS), lambda s, f: (0, s, 0, 0)),
            ],
            out_specs=[
                pl.BlockSpec((1, CELLS, CELLS * CELLS), lambda s, f: (s, 0, 0)),
                pl.BlockSpec((3, 1, CELLS, CELLS * CELLS), lambda s, f: (0, s, 0, 0)),
            ],
            scratch_shapes=[pltpu.VMEM((slots * 40, 2 * LANES), jnp.float32)],
        ),
        out_shape=[
            jax.ShapeDtypeStruct(density.shape, jnp.float32),
            jax.ShapeDtypeStruct(velocity.shape, jnp.float32),
        ],
        compiler_params=pltpu.CompilerParams(vmem_limit_bytes=48 << 20),
        name="relax_and_kick",
    )(flags, patch, block_rows, table, density, low, high, velocity)


def local(root_density, subgrid_density, velocity, slot_anchor, slot_count, neighbour):
    place_first = lax.axis_index("px")
    place_second = lax.axis_index("py")
    device = place_first * PY + place_second
    slots = subgrid_density.shape[0]
    q, eig = fourier_basis()
    basis = jnp.asarray(q, jnp.float32)
    eigen = jnp.asarray(eig, jnp.float32)
    low = from_behind(subgrid_density[:, :, -EDGE * CELLS:], "py", 1)
    high = from_behind(subgrid_density[:, :, :EDGE * CELLS], "py", -1)

    packed = jnp.einsum("xyz,zmt->tmyx", root_density, basis.reshape(NR, MODES, DEV), precision=HIGH)
    got = lax.all_to_all(packed.reshape(DEV, MODES * YB * XB), ("px", "py"), 0, 0, tiled=True)
    own_eig = eigen[jnp.arange(MODES) * DEV + device]
    back = lax.all_to_all(solve_planes(own_eig, got, q, eig), ("px", "py"), 0, 0, tiled=True)

    targets = jnp.arange(PY, dtype=jnp.int32)
    wanted = (place_first * PY + targets) * slots + (place_second - targets) % PY
    anchors = slot_anchor[:, wanted]
    third = (anchors[2][:, None] - 1 + jnp.arange(16, dtype=jnp.int32)[None, :]) % NR
    columns = basis[third.reshape(-1)].T
    start_first = jnp.clip(anchors[0] - place_first * XB, 0, XB - REG)
    start_second = jnp.clip(anchors[1] - place_second * YB, 0, YB - REG)
    sending = cut_patches(back, columns, jnp.stack([start_first, start_second]))
    arrived = lax.all_to_all(sending, "py", 0, 0, tiled=True)
    positions = jnp.arange(slots, dtype=jnp.int32)

    coarse_potential = block_of(back, q)

    first_slot = device * slots
    padded = jnp.pad(neighbour, ((0, 0), (slots, slots)), constant_values=-1)
    nearby = lax.dynamic_slice_in_dim(neighbour, first_slot, slots, 1)
    below = lax.dynamic_slice_in_dim(padded, first_slot, slots, 1)
    above = lax.dynamic_slice_in_dim(padded, first_slot + 2 * slots, slots, 1)
    flags = jnp.stack([
        nearby[0] >= 0, nearby[1] >= 0, below[1] >= 0, above[0] >= 0,
        positions < slot_count[device], (place_second + positions) % PY,
    ], axis=1).astype(jnp.int32)
    subgrid_potential, kicked = relax(flags, arrived, subgrid_density, low, high, velocity)
    return coarse_potential, subgrid_potential, kicked


def solution(mesh):
    return jax.shard_map(
        local,
        mesh=mesh,
        in_specs=(
            P("px", "py", None),
            P(("px", "py"), None, None),
            P(None, ("px", "py"), None, None),
            P(),
            P(),
            P(),
        ),
        out_specs=(
            P("px", "py", None),
            P(("px", "py"), None, None),
            P(None, ("px", "py"), None, None),
        ),
        check_vma=False,
    )
```

```python
import ml_dtypes
import numpy as np
import jax
import jax.numpy as jnp
from jax import lax
from jax.experimental import pallas as pl
from jax.experimental.pallas import tpu as pltpu
from jax.sharding import PartitionSpec as P

NR = 384
REG = 8
REF = 4
SWEEPS = 4
CELLS = REG * REF
PX = 8
PY = 16
DEV = PX * PY
MODES = NR // DEV
XB = NR // PX
YB = NR // PY
XE = XB + 2
YE = YB + 4
PLANE = 1408
ROWS = 48
TILES_IN = XB * YB // 128
TILES_OUT = PLANE // 128
EDGE = 4
LANES = (CELLS + 2 * EDGE) * CELLS
RELAX = 6.0 / 7.0
HIGH = lax.Precision.HIGH


def fourier_basis():
    n = np.arange(NR)
    k = np.concatenate([[0, NR // 2], np.repeat(np.arange(1, NR // 2), 2)])
    phase = 2.0 * np.pi * ((n[:, None] * k[None, :]) % NR) / NR
    odd = np.zeros(NR, bool)
    odd[3::2] = True
    q = np.where(odd[None, :], np.sin(phase), np.cos(phase)) * np.sqrt(2.0 / NR)
    q[:, :2] *= np.sqrt(0.5)
    eig = -4.0 * np.sin(np.pi * k / NR) ** 2
    return q, eig


def line_weights(first, last, offset):
    cells = np.arange(first, last)
    marks = 2 * cells + 1 - REF
    low = marks // (2 * REF)
    frac = (marks - 2 * REF * low) / (2.0 * REF)
    table = np.zeros((len(cells), 16))
    rows = np.arange(len(cells))
    table[rows, low + offset] += 1.0 - frac
    table[rows, low + 1 + offset] += frac
    return table


def interpolation_tables():
    wi = line_weights(0, CELLS, 1)[:, :10]
    wlow = line_weights(-1, 0, 1)[:, :10]
    whigh = line_weights(CELLS, CELLS + 1, 1)[:, :10]
    wj = line_weights(-EDGE, CELLS + EDGE, 2)[:, :12]
    jlow = line_weights(-EDGE - 1, -EDGE, 2)[0, :12]
    jhigh = line_weights(CELLS + EDGE, CELLS + EDGE + 1, 2)[0, :12]
    inner = np.einsum("jb,kc->bcjk", wj, wi)
    edge = np.zeros_like(inner)
    edge[:, :, :, 0] += np.einsum("jb,c->bcj", wj, wlow[0])
    edge[:, :, :, -1] += np.einsum("jb,c->bcj", wj, whigh[0])
    edge[:, :, 0, :] += np.einsum("b,kc->bck", jlow, wi)
    edge[:, :, -1, :] += np.einsum("b,kc->bck", jhigh, wi)
    cols = np.zeros((128, 2 * LANES))
    cols[:120, :LANES] = inner.reshape(120, LANES)
    cols[:120, LANES:] = edge.reshape(120, LANES)
    rows = np.zeros((40, 16))
    rows[:32, :10] = wi
    rows[32, :10] = wlow[0]
    rows[33, :10] = whigh[0]
    return rows, cols


def from_behind(value, axis, steps):
    count = lax.axis_size(axis)
    initial, last = (max(0, -steps), min(count, count - steps))
    return lax.ppermute(value, axis, [(source, source + steps) for source in range(initial, last)])


def split3(x):
    hi = x.astype(jnp.bfloat16)
    rest = x - hi.astype(jnp.float32)
    mid = rest.astype(jnp.bfloat16)
    low = (rest - mid.astype(jnp.float32)).astype(jnp.bfloat16)
    return hi, mid, low


def dot(a, b):
    return jnp.dot(a, b, preferred_element_type=jnp.float32)


def split2(x):
    hi = x.astype(jnp.bfloat16)
    return hi, (x - hi.astype(jnp.float32)).astype(jnp.bfloat16)


def table_pair(table):
    hi = np.asarray(table, np.float32).astype(ml_dtypes.bfloat16)
    low = (np.asarray(table) - hi.astype(np.float64)).astype(ml_dtypes.bfloat16)
    return jnp.asarray(np.stack([hi, low]))


def right_product(x, pair):
    hi, low = split2(x)
    return dot(hi, pair[0]) + dot(low, pair[0]) + dot(hi, pair[1])


def left_product(pair, x):
    hi, low = split2(x)
    return dot(pair[0], hi) + dot(pair[0], low) + dot(pair[1], hi)


def moved(tiles, source, target, width, lane, out):
    shift = (target - source) % 128
    rolled = {}
    begin = 0
    while begin < width:
        src, dst = source + begin, target + begin
        end = min(width, begin + 128 - src % 128, begin + 128 - dst % 128)
        if src // 128 not in rolled:
            tile = tiles(src // 128)
            rolled[src // 128] = pltpu.roll(tile, shift, 1) if shift else tile
        tile = rolled[src // 128]
        first, last = dst % 128, dst % 128 + end - begin
        old = out[dst // 128]
        if old is None or first == 0:
            out[dst // 128] = tile
        else:
            out[dst // 128] = jnp.where(lane >= first, tile, old)
        begin = end


def forward_kernel(in_ref, q_ref, out_ref, rows_ref, sem):
    copies = [pltpu.make_async_copy(in_ref.at[:, y], rows_ref.at[y], sem.at[y]) for y in range(YB)]
    for copy in copies:
        copy.start()
    for copy in copies:
        copy.wait()
    hi, low = split2(rows_ref[...].reshape(YB * XB, NR))
    contract = (((1,), (1,)), ((), ()))
    modes = None
    for left, right in ((q_ref[0], hi), (q_ref[0], low), (q_ref[1], hi)):
        part = lax.dot_general(left, right, contract, preferred_element_type=jnp.float32)
        modes = part if modes is None else modes + part
    for m in range(MODES):
        for c in range(TILES_IN):
            out_ref[pl.ds(m * TILES_IN + c, DEV, stride=MODES * TILES_IN), :] = (
                modes[m * DEV:(m + 1) * DEV, c * 128:(c + 1) * 128])


def forward_third(density, q):
    return pl.pallas_call(
        forward_kernel,
        out_shape=jax.ShapeDtypeStruct((DEV * MODES * TILES_IN, 128), jnp.float32),
        in_specs=[pl.BlockSpec(memory_space=pl.ANY), pl.BlockSpec(memory_space=pltpu.VMEM)],
        out_specs=pl.BlockSpec(memory_space=pltpu.VMEM),
        scratch_shapes=[pltpu.VMEM((YB, XB, NR), jnp.float32), pltpu.SemaphoreType.DMA((YB,))],
        compiler_params=pltpu.CompilerParams(vmem_limit_bytes=48 << 20),
        name="forward_third",
    )(density, table_pair(q.T))


def plane_kernel(mode_ref, in_ref, ax_ref, ay_ref, by_ref, bx_ref, ey_ref, ex_ref, out_ref, x_ref, o_ref):
    lane = lax.broadcasted_iota(jnp.int32, (8, 128), 1)
    stride_in = MODES * TILES_IN
    stride_out = MODES * TILES_OUT
    for m in range(MODES):
        for y in range(YB):
            for h in range(2):
                even, odd = [None, None], [None, None]
                for p in range(PX // 2):
                    loaded = {}

                    def pair(c):
                        if c not in loaded:
                            near = in_ref[pl.ds((p * PY + h * 8) * stride_in + m * TILES_IN + c, 8, stride=stride_in), :]
                            far = in_ref[pl.ds(((p + PX // 2) * PY + h * 8) * stride_in + m * TILES_IN + c, 8,
                                               stride=stride_in), :]
                            loaded[c] = (near + far, near - far)
                        return loaded[c]

                    moved(lambda c: pair(c)[0], y * XB, p * XB, XB, lane, even)
                    moved(lambda c: pair(c)[1], y * XB, p * XB, XB, lane, odd)
                row = y * PY + h * 8
                for t, tile in enumerate(even + odd):
                    x_ref[m, row:row + 8, t * 128:(t + 1) * 128] = tile
    for m in range(MODES):
        z = jnp.concatenate([right_product(x_ref[m, :, i * 256:(i + 1) * 256], ax_ref.at[i]) for i in range(2)], axis=1)
        z = z.reshape(YB, PY, 512)
        near = z[:, :8].reshape(YB * 8, 512)
        far = z[:, 8:].reshape(YB * 8, 512)
        halves = []
        for i, z in enumerate((near + far, near - far)):
            z = left_product(ay_ref.at[i], z)
            total = mode_ref[m] + ey_ref[i] + ex_ref[...]
            is_zero = total == 0.0
            z = jnp.where(is_zero, 0.0, z / jnp.where(is_zero, -1.0, total))
            halves.append(left_product(by_ref.at[i], z))
        z = jnp.concatenate([halves[0] + halves[1], halves[0] - halves[1]], axis=0)
        even, odd = (right_product(z[:, i * 256:(i + 1) * 256], bx_ref.at[i]) for i in range(2))
        o_ref[m, :, :256] = even + odd
        o_ref[m, :, 256:] = even - odd
    for m in range(MODES):
        for p in range(PX):
            for h in range(2):
                out = [None] * TILES_OUT
                for y in range(YE):
                    row = h * YE * 8 + y * 8
                    moved(lambda t: o_ref[m, row:row + 8, t * 128:(t + 1) * 128], p * 64, y * XE, XE, lane, out)
                for t in range(TILES_OUT):
                    out_ref[pl.ds((p * PY + h * 8) * stride_out + m * TILES_OUT + t, 8, stride=stride_out), :] = out[t]


def solve_planes(own_eig, got, q, eig):
    k = np.rint(np.arcsin(np.sqrt(-eig / 4.0)) * NR / np.pi).astype(int)
    n = np.arange(NR // 2)
    order = (n % 8) * YB + n // 8
    wide = ((np.arange(YE)[:, None] - 2 + np.arange(8)[None, :] * YB) % NR).reshape(-1)
    half = NR // 2
    tables = [[], [], [], []]
    ey = np.zeros((2, half, 1))
    ex = np.full((1, 512), -1.0)
    for i in range(2):
        part = q[:, k % 2 == i]
        ey[i, :, 0] = eig[k % 2 == i]
        ex[0, i * 256:i * 256 + half] = eig[k % 2 == i]
        ax = np.zeros((256, 256))
        ax[:half, :half] = part[:half]
        bx = np.zeros((256, PX // 2, 64))
        for p in range(PX // 2):
            bx[:half, p, :XE] = part[(p * XB + np.arange(XE) - 1) % NR].T
        for bucket, table in zip(tables, (ax, part[order].T, part[wide], bx.reshape(256, 256))):
            bucket.append(table_pair(table))
    tables = [jnp.stack(bucket) for bucket in tables]
    vmem = pl.BlockSpec(memory_space=pltpu.VMEM)
    return pl.pallas_call(
        plane_kernel,
        out_shape=jax.ShapeDtypeStruct((DEV * MODES * TILES_OUT, 128), jnp.float32),
        in_specs=[pl.BlockSpec(memory_space=pltpu.SMEM)] + [vmem] * 7,
        out_specs=vmem,
        scratch_shapes=[pltpu.VMEM((MODES, NR, 512), jnp.float32), pltpu.VMEM((MODES, YE * PY, 512), jnp.float32)],
        compiler_params=pltpu.CompilerParams(vmem_limit_bytes=48 << 20),
        name="solve_planes",
    )(own_eig, got, *tables, jnp.asarray(ey, jnp.float32), jnp.asarray(ex, jnp.float32))


def columns_of(s_ref, pair):
    total = None
    for m in range(MODES):
        rows = jnp.concatenate(
            [s_ref[pl.ds(m * TILES_OUT + c, DEV, stride=MODES * TILES_OUT), :] for c in range(TILES_OUT)], axis=1)
        hi, low = split2(rows)
        rows = slice(m * DEV, (m + 1) * DEV)
        for left, right in ((hi, pair[0, rows]), (low, pair[0, rows]), (hi, pair[1, rows])):
            part = lax.dot_general(left, right, (((0,), (0,)), ((), ())), preferred_element_type=jnp.float32)
            total = part if total is None else total + part
    return total


def cut_kernel(start_ref, s_ref, g_ref, out_ref, p_ref):
    cells = columns_of(s_ref, jnp.stack(split2(g_ref[...])))
    for y in range(YE):
        p_ref[y, :XE, :] = cells[y * XE:(y + 1) * XE, :]
    lane = lax.broadcasted_iota(jnp.int32, (16, 128), 1)
    inside = lax.broadcasted_iota(jnp.int32, (16, 128), 0) < REG + 2
    for t in range(PY):
        acc = jnp.zeros((16, 128), jnp.float32)
        for b in range(12):
            first = pl.multiple_of(start_ref[0, t], 8)
            tile = p_ref[start_ref[1, t] + b, pl.ds(first, 16), (t // 8) * 128:(t // 8 + 1) * 128]
            shift = (b * 10 - (t % 8) * 16) % 128
            if shift:
                tile = pltpu.roll(tile, shift, 1)
            acc = jnp.where((lane >= b * 10) & (lane < b * 10 + 10) & inside, tile, acc)
        out_ref[t * 16:(t + 1) * 16, :] = acc


def cut_patches(spectrum, columns, starts):
    return pl.pallas_call(
        cut_kernel,
        out_shape=jax.ShapeDtypeStruct((PY * 16, 128), jnp.float32),
        in_specs=[pl.BlockSpec(memory_space=pltpu.SMEM),
                  pl.BlockSpec(memory_space=pltpu.VMEM),
                  pl.BlockSpec(memory_space=pltpu.VMEM)],
        out_specs=pl.BlockSpec(memory_space=pltpu.VMEM),
        scratch_shapes=[pltpu.VMEM((YE, 56, 256), jnp.float32)],
        compiler_params=pltpu.CompilerParams(vmem_limit_bytes=48 << 20),
        name="cut_patches",
    )(starts, spectrum, columns)


def block_kernel(s_ref, q_ref, out_ref):
    cells = columns_of(s_ref, q_ref)
    for y in range(YB):
        first = (y + 2) * XE + 1
        out_ref[:, y, :] = cells[first:first + XB, :]


def block_of(spectrum, q):
    return pl.pallas_call(
        block_kernel,
        out_shape=jax.ShapeDtypeStruct((XB, YB, NR), jnp.float32),
        in_specs=[pl.BlockSpec(memory_space=pltpu.VMEM), pl.BlockSpec(memory_space=pltpu.VMEM)],
        out_specs=pl.BlockSpec(memory_space=pltpu.VMEM),
        compiler_params=pltpu.CompilerParams(vmem_limit_bytes=48 << 20),
        name="block_of",
    )(spectrum, table_pair(q.T))


def relax_kernel(flag_ref, patch_ref, rows_ref, cols_ref, dens_ref, low_ref, high_ref, vel_ref,
                 pot_ref, out_ref, grid_ref, v_ref, f_ref):
    step = pl.program_id(0)

    @pl.when(step == 0)
    def _():
        rows = rows_ref[...]
        ordered = jnp.concatenate(
            [patch_ref[pl.ds(pl.multiple_of(flag_ref[j, 5] * 16, 16), 16), :] for j in range(PY)], axis=0)
        expanded = jnp.zeros((640, 128), jnp.float32)
        for part in split3(ordered):
            expanded += dot(rows, part)
        pair = jnp.concatenate(split2(expanded), axis=1)
        for n in range(0, 2 * LANES, 256):
            grid_ref[:, n:n + 256] = dot(pair, cols_ref[:, n:n + 256])

    base = pl.multiple_of(step * 40, 8)
    tiles = LANES // 128
    lane = lax.broadcasted_iota(jnp.int32, (8, 128), 1)
    third_first = lane % CELLS == 0
    third_last = lane % CELLS == CELLS - 1
    second_first = lane < CELLS
    second_last = lane >= 128 - CELLS
    zero = jnp.zeros((8, 128), jnp.float32)
    use_low = jnp.broadcast_to(flag_ref[step, 0], (8, 128)) > 0
    use_high = jnp.broadcast_to(flag_ref[step, 1], (8, 128)) > 0
    same_low = jnp.broadcast_to(flag_ref[step, 2], (8, 128)) > 0
    same_high = jnp.broadcast_to(flag_ref[step, 3], (8, 128)) > 0
    live = jnp.broadcast_to(flag_ref[step, 4], (8, 128)) > 0

    def start(t, r):
        return grid_ref[pl.ds(base + r * 8, 8), t * 128:(t + 1) * 128]

    def edge(t, r):
        return grid_ref[pl.ds(base + r * 8, 8), LANES + t * 128:LANES + (t + 1) * 128]

    def row_of(slot, t, r):
        return (slot * tiles + t) * ROWS + 8 + r * 8

    for t in range(tiles):
        faces = grid_ref[pl.ds(base + 32, 8), t * 128:(t + 1) * 128]
        for slot in range(2):
            row = row_of(slot, t, 0)
            v_ref[row - 1:row, :] = faces[0:1]
            v_ref[row + CELLS:row + CELLS + 1, :] = faces[1:2]
        for r in range(4):
            rows = slice(r * 8, r * 8 + 8)
            if t == 0:
                rho = low_ref[0, rows, :]
            elif t == tiles - 1:
                rho = high_ref[0, rows, :]
            else:
                rho = dens_ref[0, rows, (t - 1) * 128:t * 128]
            f_ref[t, r] = edge(t, r) - rho * (1.0 / (REF * REF))
            row = row_of(0, t, r)
            v_ref[row:row + 8, :] = start(t, r)

    def second_neighbours(value, t, r):
        here = value(t, r)
        if t == 0:
            before = zero
        else:
            before = pltpu.roll(value(t - 1, r), CELLS, 1)
            if t == tiles - 1:
                before = jnp.where(same_high, before, pltpu.roll(start(t - 1, r), CELLS, 1))
        if t == tiles - 1:
            after = zero
        else:
            after = pltpu.roll(value(t + 1, r), 128 - CELLS, 1)
            if t == 0:
                after = jnp.where(same_low, after, pltpu.roll(start(t + 1, r), 128 - CELLS, 1))
        return (jnp.where(second_first, before, pltpu.roll(here, CELLS, 1)),
                jnp.where(second_last, after, pltpu.roll(here, 128 - CELLS, 1)))

    def first_neighbours(slot, t, r):
        row = row_of(slot, t, r)
        return v_ref[row - 1:row + 7, :], v_ref[row + 1:row + 9, :]

    def third_neighbours(here, low, high):
        return (jnp.where(third_first, low, pltpu.roll(here, 1, 1)),
                jnp.where(third_last, high, pltpu.roll(here, 127, 1)))

    def reader(slot):
        return lambda t, r: v_ref[row_of(slot, t, r):row_of(slot, t, r) + 8, :]

    for sweep in range(SWEEPS):
        slot = sweep % 2
        value = reader(slot)
        for r in range(4):
            for t in range(tiles):
                here = value(t, r)
                before, after = second_neighbours(value, t, r)
                total = here + f_ref[t, r] + (before + after)
                before, after = first_neighbours(slot, t, r)
                total += before + after
                before, after = third_neighbours(here, zero, zero)
                total += before + after
                new = total * (1.0 - RELAX)
                if t == 0:
                    new = jnp.where(use_low, new, here)
                if t == tiles - 1:
                    new = jnp.where(use_high, new, here)
                row = row_of(1 - slot, t, r)
                v_ref[row:row + 8, :] = new

    slot = SWEEPS % 2
    value = reader(slot)
    for r in range(4):
        for t in range(1, tiles - 1):
            here = value(t, r)
            rows = slice(r * 8, r * 8 + 8)
            cols = slice((t - 1) * 128, t * 128)
            pot_ref[0, rows, cols] = jnp.where(live, here, 0.0)
            wall = edge(t, r)
            pairs = (first_neighbours(slot, t, r), second_neighbours(value, t, r), third_neighbours(here, wall, wall))
            for q, (before, after) in enumerate(pairs):
                out_ref[q, 0, rows, cols] = jnp.where(live, vel_ref[q, 0, rows, cols] - (after - before) * (REF / 2.0), 0.0)


def relax(flags, patch, density, low, high, velocity):
    slots = density.shape[0]
    rows, cols = interpolation_tables()
    block_rows = jnp.asarray(np.kron(np.eye(slots), rows), jnp.bfloat16)
    table = jnp.asarray(np.concatenate([cols, cols]), jnp.bfloat16)
    whole = lambda shape: pl.BlockSpec(shape, lambda s, f: (0,) * len(shape), pipeline_mode=pl.Buffered(1))
    return pl.pallas_call(
        relax_kernel,
        grid_spec=pltpu.PrefetchScalarGridSpec(
            num_scalar_prefetch=1,
            grid=(slots,),
            in_specs=[
                whole((slots * 16, 128)),
                whole((slots * 40, slots * 16)),
                whole((256, 2 * LANES)),
                pl.BlockSpec((1, CELLS, CELLS * CELLS), lambda s, f: (s, 0, 0)),
                pl.BlockSpec((1, CELLS, EDGE * CELLS), lambda s, f: (s, 0, 0)),
                pl.BlockSpec((1, CELLS, EDGE * CELLS), lambda s, f: (s, 0, 0)),
                pl.BlockSpec((3, 1, CELLS, CELLS * CELLS), lambda s, f: (0, s, 0, 0)),
            ],
            out_specs=[
                pl.BlockSpec((1, CELLS, CELLS * CELLS), lambda s, f: (s, 0, 0)),
                pl.BlockSpec((3, 1, CELLS, CELLS * CELLS), lambda s, f: (0, s, 0, 0)),
            ],
            scratch_shapes=[
                pltpu.VMEM((slots * 40, 2 * LANES), jnp.float32),
                pltpu.VMEM((2 * (LANES // 128) * ROWS, 128), jnp.float32),
                pltpu.VMEM((LANES // 128, 4, 8, 128), jnp.float32),
            ],
        ),
        out_shape=[
            jax.ShapeDtypeStruct(density.shape, jnp.float32),
            jax.ShapeDtypeStruct(velocity.shape, jnp.float32),
        ],
        compiler_params=pltpu.CompilerParams(vmem_limit_bytes=48 << 20),
        name="relax_and_kick",
    )(flags, patch, block_rows, table, density, low, high, velocity)


def local(root_density, subgrid_density, velocity, slot_anchor, slot_count, neighbour):
    place_first = lax.axis_index("px")
    place_second = lax.axis_index("py")
    device = place_first * PY + place_second
    slots = subgrid_density.shape[0]
    q, eig = fourier_basis()
    basis = jnp.asarray(q, jnp.float32)
    eigen = jnp.asarray(eig, jnp.float32)
    low = from_behind(subgrid_density[:, :, -EDGE * CELLS:], "py", 1)
    high = from_behind(subgrid_density[:, :, :EDGE * CELLS], "py", -1)

    packed = forward_third(root_density, q).reshape(DEV, 1, MODES * YB * XB)
    got = lax.all_to_all(packed, ("px", "py"), 0, 0, tiled=True).reshape(-1, 128)
    own_eig = eigen[jnp.arange(MODES) * DEV + device]
    solved = solve_planes(own_eig, got, q, eig).reshape(DEV, 1, MODES * PLANE)
    back = lax.all_to_all(solved, ("px", "py"), 0, 0, tiled=True).reshape(-1, 128)

    targets = jnp.arange(PY, dtype=jnp.int32)
    wanted = (place_first * PY + targets) * slots + (place_second - targets) % PY
    anchors = slot_anchor[:, wanted]
    third = (anchors[2][:, None] - 1 + jnp.arange(16, dtype=jnp.int32)[None, :]) % NR
    columns = basis[third.reshape(-1)].T
    start_first = jnp.clip(anchors[0] - place_first * XB, 0, XB - REG)
    start_second = jnp.clip(anchors[1] - place_second * YB, 0, YB - REG)
    sending = cut_patches(back, columns, jnp.stack([start_first, start_second]))
    arrived = lax.all_to_all(sending, "py", 0, 0, tiled=True)
    positions = jnp.arange(slots, dtype=jnp.int32)

    coarse_potential = block_of(back, q)

    first_slot = device * slots
    padded = jnp.pad(neighbour, ((0, 0), (slots, slots)), constant_values=-1)
    nearby = lax.dynamic_slice_in_dim(neighbour, first_slot, slots, 1)
    below = lax.dynamic_slice_in_dim(padded, first_slot, slots, 1)
    above = lax.dynamic_slice_in_dim(padded, first_slot + 2 * slots, slots, 1)
    flags = jnp.stack([
        nearby[0] >= 0, nearby[1] >= 0, below[1] >= 0, above[0] >= 0,
        positions < slot_count[device], (place_second + positions) % PY,
    ], axis=1).astype(jnp.int32)
    subgrid_potential, kicked = relax(flags, arrived, subgrid_density, low, high, velocity)
    return coarse_potential, subgrid_potential, kicked


def solution(mesh):
    return jax.shard_map(
        local,
        mesh=mesh,
        in_specs=(
            P("px", "py", None),
            P(("px", "py"), None, None),
            P(None, ("px", "py"), None, None),
            P(),
            P(),
            P(),
        ),
        out_specs=(
            P("px", "py", None),
            P(("px", "py"), None, None),
            P(None, ("px", "py"), None, None),
        ),
        check_vma=False,
    )
```

```python
import ml_dtypes
import numpy as np
import jax
import jax.numpy as jnp
from jax import lax
from jax.experimental import pallas as pl
from jax.experimental.pallas import tpu as pltpu
from jax.sharding import PartitionSpec as P

NR = 384
REG = 8
REF = 4
SWEEPS = 4
CELLS = REG * REF
PX = 8
PY = 16
DEV = PX * PY
MODES = NR // DEV
XB = NR // PX
YB = NR // PY
XE = XB + 2
YE = YB + 4
PLANE = 1408
ROWS = 48
TILES_IN = XB * YB // 128
TILES_OUT = PLANE // 128
EDGE = 4
LANES = (CELLS + 2 * EDGE) * CELLS
RELAX = 6.0 / 7.0
HIGH = lax.Precision.HIGH


def fourier_basis():
    n = np.arange(NR)
    k = np.concatenate([[0, NR // 2], np.repeat(np.arange(1, NR // 2), 2)])
    phase = 2.0 * np.pi * ((n[:, None] * k[None, :]) % NR) / NR
    odd = np.zeros(NR, bool)
    odd[3::2] = True
    q = np.where(odd[None, :], np.sin(phase), np.cos(phase)) * np.sqrt(2.0 / NR)
    q[:, :2] *= np.sqrt(0.5)
    eig = -4.0 * np.sin(np.pi * k / NR) ** 2
    return q, eig


def line_weights(first, last, offset):
    cells = np.arange(first, last)
    marks = 2 * cells + 1 - REF
    low = marks // (2 * REF)
    frac = (marks - 2 * REF * low) / (2.0 * REF)
    table = np.zeros((len(cells), 16))
    rows = np.arange(len(cells))
    table[rows, low + offset] += 1.0 - frac
    table[rows, low + 1 + offset] += frac
    return table


def interpolation_tables():
    wi = line_weights(0, CELLS, 1)[:, :10]
    wlow = line_weights(-1, 0, 1)[:, :10]
    whigh = line_weights(CELLS, CELLS + 1, 1)[:, :10]
    wj = line_weights(-EDGE, CELLS + EDGE, 2)[:, :12]
    jlow = line_weights(-EDGE - 1, -EDGE, 2)[0, :12]
    jhigh = line_weights(CELLS + EDGE, CELLS + EDGE + 1, 2)[0, :12]
    inner = np.einsum("jb,kc->bcjk", wj, wi)
    edge = np.zeros_like(inner)
    edge[:, :, :, 0] += np.einsum("jb,c->bcj", wj, wlow[0])
    edge[:, :, :, -1] += np.einsum("jb,c->bcj", wj, whigh[0])
    edge[:, :, 0, :] += np.einsum("b,kc->bck", jlow, wi)
    edge[:, :, -1, :] += np.einsum("b,kc->bck", jhigh, wi)
    cols = np.zeros((128, 2 * LANES))
    cols[:120, :LANES] = inner.reshape(120, LANES)
    cols[:120, LANES:] = edge.reshape(120, LANES)
    rows = np.zeros((40, 16))
    rows[:32, :10] = wi
    rows[32, :10] = wlow[0]
    rows[33, :10] = whigh[0]
    return rows, cols


def from_behind(value, axis, steps):
    count = lax.axis_size(axis)
    initial, last = (max(0, -steps), min(count, count - steps))
    return lax.ppermute(value, axis, [(source, source + steps) for source in range(initial, last)])


def in_hbm(x):
    return pltpu.with_memory_space_constraint(x, pltpu.HBM)


def in_vmem(x):
    return pltpu.with_memory_space_constraint(x, pltpu.VMEM)


def split3(x):
    hi = x.astype(jnp.bfloat16)
    rest = x - hi.astype(jnp.float32)
    mid = rest.astype(jnp.bfloat16)
    low = (rest - mid.astype(jnp.float32)).astype(jnp.bfloat16)
    return hi, mid, low


def dot(a, b):
    return jnp.dot(a, b, preferred_element_type=jnp.float32)


def split2(x):
    hi = x.astype(jnp.bfloat16)
    return hi, (x - hi.astype(jnp.float32)).astype(jnp.bfloat16)


def table_pair(table):
    hi = np.asarray(table, np.float32).astype(ml_dtypes.bfloat16)
    low = (np.asarray(table) - hi.astype(np.float64)).astype(ml_dtypes.bfloat16)
    return jnp.asarray(np.stack([hi, low]))


def right_product(x, pair):
    hi, low = split2(x)
    return dot(hi, pair[0]) + dot(low, pair[0]) + dot(hi, pair[1])


def left_product(pair, x):
    hi, low = split2(x)
    return dot(pair[0], hi) + dot(pair[0], low) + dot(pair[1], hi)


def moved(tiles, source, target, width, lane, out):
    shift = (target - source) % 128
    rolled = {}
    begin = 0
    while begin < width:
        src, dst = source + begin, target + begin
        end = min(width, begin + 128 - src % 128, begin + 128 - dst % 128)
        if src // 128 not in rolled:
            tile = tiles(src // 128)
            rolled[src // 128] = pltpu.roll(tile, shift, 1) if shift else tile
        tile = rolled[src // 128]
        first, last = dst % 128, dst % 128 + end - begin
        old = out[dst // 128]
        if old is None or first == 0:
            out[dst // 128] = tile
        else:
            out[dst // 128] = jnp.where(lane >= first, tile, old)
        begin = end


def forward_kernel(in_ref, q_hbm, out_ref, rows_ref, q_ref, sem):
    copies = [pltpu.make_async_copy(in_ref.at[:, y], rows_ref.at[y], sem.at[y]) for y in range(YB)]
    table = pltpu.make_async_copy(q_hbm, q_ref, sem.at[YB])
    table.start()
    for copy in copies:
        copy.start()
    table.wait()
    contract = (((1,), (1,)), ((), ()))
    for part in range(3):
        for copy in copies[part * 8:(part + 1) * 8]:
            copy.wait()
        hi, low = split2(rows_ref[part * 8:(part + 1) * 8].reshape(8 * XB, NR))
        modes = None
        for left, right in ((q_ref[0], hi), (q_ref[0], low), (q_ref[1], hi)):
            term = lax.dot_general(left, right, contract, preferred_element_type=jnp.float32)
            modes = term if modes is None else modes + term
        for m in range(MODES):
            for c in range(3):
                out_ref[pl.ds(m * TILES_IN + part * 3 + c, DEV, stride=MODES * TILES_IN), :] = (
                    modes[m * DEV:(m + 1) * DEV, c * 128:(c + 1) * 128])


def forward_third(density, q):
    return pl.pallas_call(
        forward_kernel,
        out_shape=pltpu.HBM((DEV * MODES * TILES_IN, 128), jnp.float32),
        in_specs=[pl.BlockSpec(memory_space=pltpu.HBM), pl.BlockSpec(memory_space=pltpu.HBM)],
        out_specs=pl.BlockSpec(memory_space=pltpu.VMEM),
        scratch_shapes=[pltpu.VMEM((YB, XB, NR), jnp.float32), pltpu.VMEM((2, NR, NR), jnp.bfloat16),
                        pltpu.SemaphoreType.DMA((YB + 1,))],
        compiler_params=pltpu.CompilerParams(vmem_limit_bytes=16 << 20),
        name="forward_third",
    )(in_hbm(density), in_hbm(table_pair(q.T)))


def plane_kernel(mode_ref, in_ref, ax_ref, ay_ref, by_ref, bx_ref, ey_ref, ex_ref, out_ref, x_ref, o_ref):
    lane = lax.broadcasted_iota(jnp.int32, (8, 128), 1)
    stride_in = MODES * TILES_IN
    stride_out = MODES * TILES_OUT
    for m in range(MODES):
        for y in range(YB):
            for h in range(2):
                even, odd = [None, None], [None, None]
                for p in range(PX // 2):
                    loaded = {}

                    def pair(c):
                        if c not in loaded:
                            near = in_ref[pl.ds((p * PY + h * 8) * stride_in + m * TILES_IN + c, 8, stride=stride_in), :]
                            far = in_ref[pl.ds(((p + PX // 2) * PY + h * 8) * stride_in + m * TILES_IN + c, 8,
                                               stride=stride_in), :]
                            loaded[c] = (near + far, near - far)
                        return loaded[c]

                    moved(lambda c: pair(c)[0], y * XB, p * XB, XB, lane, even)
                    moved(lambda c: pair(c)[1], y * XB, p * XB, XB, lane, odd)
                row = y * PY + h * 8
                for t, tile in enumerate(even + odd):
                    x_ref[m, row:row + 8, t * 128:(t + 1) * 128] = tile
    for m in range(MODES):
        z = jnp.concatenate([right_product(x_ref[m, :, i * 256:(i + 1) * 256], ax_ref.at[i]) for i in range(2)], axis=1)
        z = z.reshape(YB, PY, 512)
        near = z[:, :8].reshape(YB * 8, 512)
        far = z[:, 8:].reshape(YB * 8, 512)
        halves = []
        for i, z in enumerate((near + far, near - far)):
            z = left_product(ay_ref.at[i], z)
            total = mode_ref[m] + ey_ref[i] + ex_ref[...]
            is_zero = total == 0.0
            z = jnp.where(is_zero, 0.0, z / jnp.where(is_zero, -1.0, total))
            halves.append(left_product(by_ref.at[i], z))
        z = jnp.concatenate([halves[0] + halves[1], halves[0] - halves[1]], axis=0)
        even, odd = (right_product(z[:, i * 256:(i + 1) * 256], bx_ref.at[i]) for i in range(2))
        o_ref[m, :, :256] = even + odd
        o_ref[m, :, 256:] = even - odd
    for m in range(MODES):
        for p in range(PX):
            for h in range(2):
                out = [None] * TILES_OUT
                for y in range(YE):
                    row = h * YE * 8 + y * 8
                    moved(lambda t: o_ref[m, row:row + 8, t * 128:(t + 1) * 128], p * 64, y * XE, XE, lane, out)
                for t in range(TILES_OUT):
                    out_ref[pl.ds((p * PY + h * 8) * stride_out + m * TILES_OUT + t, 8, stride=stride_out), :] = out[t]


def solve_planes(own_eig, got, q, eig):
    k = np.rint(np.arcsin(np.sqrt(-eig / 4.0)) * NR / np.pi).astype(int)
    n = np.arange(NR // 2)
    order = (n % 8) * YB + n // 8
    wide = ((np.arange(YE)[:, None] - 2 + np.arange(8)[None, :] * YB) % NR).reshape(-1)
    half = NR // 2
    tables = [[], [], [], []]
    ey = np.zeros((2, half, 1))
    ex = np.full((1, 512), -1.0)
    for i in range(2):
        part = q[:, k % 2 == i]
        ey[i, :, 0] = eig[k % 2 == i]
        ex[0, i * 256:i * 256 + half] = eig[k % 2 == i]
        ax = np.zeros((256, 256))
        ax[:half, :half] = part[:half]
        bx = np.zeros((256, PX // 2, 64))
        for p in range(PX // 2):
            bx[:half, p, :XE] = part[(p * XB + np.arange(XE) - 1) % NR].T
        for bucket, table in zip(tables, (ax, part[order].T, part[wide], bx.reshape(256, 256))):
            bucket.append(table_pair(table))
    tables = [jnp.stack(bucket) for bucket in tables]
    vmem = pl.BlockSpec(memory_space=pltpu.VMEM)
    return pl.pallas_call(
        plane_kernel,
        out_shape=pltpu.HBM((DEV * MODES * TILES_OUT, 128), jnp.float32),
        in_specs=[pl.BlockSpec(memory_space=pltpu.SMEM)] + [vmem] * 7,
        out_specs=vmem,
        scratch_shapes=[pltpu.VMEM((MODES, NR, 512), jnp.float32), pltpu.VMEM((MODES, YE * PY, 512), jnp.float32)],
        compiler_params=pltpu.CompilerParams(vmem_limit_bytes=20 << 20),
        name="solve_planes",
    )(own_eig, in_vmem(got), *tables, jnp.asarray(ey, jnp.float32), jnp.asarray(ex, jnp.float32))


def columns_of(s_ref, pair):
    total = None
    for m in range(MODES):
        rows = jnp.concatenate(
            [s_ref[pl.ds(m * TILES_OUT + c, DEV, stride=MODES * TILES_OUT), :] for c in range(TILES_OUT)], axis=1)
        hi, low = split2(rows)
        rows = slice(m * DEV, (m + 1) * DEV)
        for left, right in ((hi, pair[0, rows]), (low, pair[0, rows]), (hi, pair[1, rows])):
            part = lax.dot_general(left, right, (((0,), (0,)), ((), ())), preferred_element_type=jnp.float32)
            total = part if total is None else total + part
    return total


def cut_kernel(start_ref, s_ref, g_ref, out_ref, p_ref):
    cells = columns_of(s_ref, jnp.stack(split2(g_ref[...])))
    for y in range(YE):
        p_ref[y, :XE, :] = cells[y * XE:(y + 1) * XE, :]
    lane = lax.broadcasted_iota(jnp.int32, (16, 128), 1)
    inside = lax.broadcasted_iota(jnp.int32, (16, 128), 0) < REG + 2
    for t in range(PY):
        acc = jnp.zeros((16, 128), jnp.float32)
        for b in range(12):
            first = pl.multiple_of(start_ref[0, t], 8)
            tile = p_ref[start_ref[1, t] + b, pl.ds(first, 16), (t // 8) * 128:(t // 8 + 1) * 128]
            shift = (b * 10 - (t % 8) * 16) % 128
            if shift:
                tile = pltpu.roll(tile, shift, 1)
            acc = jnp.where((lane >= b * 10) & (lane < b * 10 + 10) & inside, tile, acc)
        out_ref[t * 16:(t + 1) * 16, :] = acc


def cut_patches(spectrum, columns, starts):
    return pl.pallas_call(
        cut_kernel,
        out_shape=jax.ShapeDtypeStruct((PY * 16, 128), jnp.float32),
        in_specs=[pl.BlockSpec(memory_space=pltpu.SMEM),
                  pl.BlockSpec(memory_space=pltpu.VMEM),
                  pl.BlockSpec(memory_space=pltpu.VMEM)],
        out_specs=pl.BlockSpec(memory_space=pltpu.VMEM),
        scratch_shapes=[pltpu.VMEM((YE, 56, 256), jnp.float32)],
        compiler_params=pltpu.CompilerParams(vmem_limit_bytes=12 << 20),
        name="cut_patches",
    )(starts, spectrum, columns)


def block_kernel(s_ref, q_ref, out_ref):
    cells = columns_of(s_ref, q_ref)
    for y in range(YB):
        first = (y + 2) * XE + 1
        out_ref[:, y, :] = cells[first:first + XB, :]


def block_of(spectrum, q):
    return pl.pallas_call(
        block_kernel,
        out_shape=jax.ShapeDtypeStruct((XB, YB, NR), jnp.float32),
        in_specs=[pl.BlockSpec(memory_space=pltpu.VMEM), pl.BlockSpec(memory_space=pltpu.VMEM)],
        out_specs=pl.BlockSpec(memory_space=pltpu.VMEM),
        compiler_params=pltpu.CompilerParams(vmem_limit_bytes=14 << 20),
        name="block_of",
    )(spectrum, table_pair(q.T))


def relax_kernel(flag_ref, patch_ref, rows_ref, cols_ref, dens_hbm, low_ref, high_ref, vel_hbm,
                 pot_hbm, out_hbm, grid_ref, v_ref, f_ref, dens_ref, vel_ref, in_sem, out_sem):
    step = pl.program_id(0)
    slots = pl.num_programs(0)

    def arrivals(s):
        return (pltpu.make_async_copy(dens_hbm.at[s], dens_ref.at[s], in_sem.at[0, s]),
                pltpu.make_async_copy(vel_hbm.at[:, s], vel_ref.at[:, s], in_sem.at[1, s]))

    def departures(s):
        return (pltpu.make_async_copy(dens_ref.at[s], pot_hbm.at[s], out_sem.at[0, s]),
                pltpu.make_async_copy(vel_ref.at[:, s], out_hbm.at[:, s], out_sem.at[1, s]))

    @pl.when(step == 0)
    def _():
        for s in range(PY):
            for copy in arrivals(s):
                copy.start()

    @pl.when(step == 0)
    def _():
        rows = rows_ref[...]
        ordered = jnp.concatenate(
            [patch_ref[pl.ds(pl.multiple_of(flag_ref[j, 5] * 16, 16), 16), :] for j in range(PY)], axis=0)
        expanded = jnp.zeros((640, 128), jnp.float32)
        for part in split3(ordered):
            expanded += dot(rows, part)
        pair = jnp.concatenate(split2(expanded), axis=1)
        for n in range(0, 2 * LANES, 256):
            table = cols_ref[:, n:n + 256]
            grid_ref[:, n:n + 256] = dot(pair, jnp.concatenate([table, table], axis=0))

    for copy in arrivals(step):
        copy.wait()
    base = pl.multiple_of(step * 40, 8)
    tiles = LANES // 128
    lane = lax.broadcasted_iota(jnp.int32, (8, 128), 1)
    third_first = lane % CELLS == 0
    third_last = lane % CELLS == CELLS - 1
    second_first = lane < CELLS
    second_last = lane >= 128 - CELLS
    zero = jnp.zeros((8, 128), jnp.float32)
    use_low = jnp.broadcast_to(flag_ref[step, 0], (8, 128)) > 0
    use_high = jnp.broadcast_to(flag_ref[step, 1], (8, 128)) > 0
    same_low = jnp.broadcast_to(flag_ref[step, 2], (8, 128)) > 0
    same_high = jnp.broadcast_to(flag_ref[step, 3], (8, 128)) > 0
    live = jnp.broadcast_to(flag_ref[step, 4], (8, 128)) > 0

    def start(t, r):
        return grid_ref[pl.ds(base + r * 8, 8), t * 128:(t + 1) * 128]

    def edge(t, r):
        return grid_ref[pl.ds(base + r * 8, 8), LANES + t * 128:LANES + (t + 1) * 128]

    def row_of(slot, t, r):
        return (slot * tiles + t) * ROWS + 8 + r * 8

    for t in range(tiles):
        faces = grid_ref[pl.ds(base + 32, 8), t * 128:(t + 1) * 128]
        for slot in range(2):
            row = row_of(slot, t, 0)
            v_ref[row - 1:row, :] = faces[0:1]
            v_ref[row + CELLS:row + CELLS + 1, :] = faces[1:2]
        for r in range(4):
            rows = slice(r * 8, r * 8 + 8)
            if t == 0:
                rho = low_ref[step, rows, :]
            elif t == tiles - 1:
                rho = high_ref[step, rows, :]
            else:
                rho = dens_ref[step, rows, (t - 1) * 128:t * 128]
            f_ref[t, r] = edge(t, r) - rho * (1.0 / (REF * REF))
            row = row_of(0, t, r)
            v_ref[row:row + 8, :] = start(t, r)

    def second_neighbours(values, r):
        up = [pltpu.roll(value, CELLS, 1) for value in values]
        down = [pltpu.roll(value, 128 - CELLS, 1) for value in values]
        into_high = jnp.where(same_high, up[-2], pltpu.roll(start(tiles - 2, r), CELLS, 1))
        into_low = jnp.where(same_low, down[1], pltpu.roll(start(1, r), 128 - CELLS, 1))
        befores = [zero] + up[:-2] + [into_high]
        afters = [into_low] + down[2:] + [zero]
        return ([jnp.where(second_first, before, here) for before, here in zip(befores, up)],
                [jnp.where(second_last, after, here) for after, here in zip(afters, down)])

    def first_neighbours(slot, t, r):
        row = row_of(slot, t, r)
        return v_ref[row - 1:row + 7, :], v_ref[row + 1:row + 9, :]

    def third_neighbours(here, low, high):
        return (jnp.where(third_first, low, pltpu.roll(here, 1, 1)),
                jnp.where(third_last, high, pltpu.roll(here, 127, 1)))

    def reader(slot):
        return lambda t, r: v_ref[row_of(slot, t, r):row_of(slot, t, r) + 8, :]

    for sweep in range(SWEEPS):
        slot = sweep % 2
        value = reader(slot)
        for r in range(4):
            values = [value(t, r) for t in range(tiles)]
            befores, afters = second_neighbours(values, r)
            for t, here in enumerate(values):
                total = here + f_ref[t, r] + (befores[t] + afters[t])
                before, after = first_neighbours(slot, t, r)
                total += before + after
                before, after = third_neighbours(here, zero, zero)
                total += before + after
                new = total * (1.0 - RELAX)
                if t == 0:
                    new = jnp.where(use_low, new, here)
                if t == tiles - 1:
                    new = jnp.where(use_high, new, here)
                row = row_of(1 - slot, t, r)
                v_ref[row:row + 8, :] = new

    slot = SWEEPS % 2
    value = reader(slot)
    for r in range(4):
        values = [value(t, r) for t in range(tiles)]
        befores, afters = second_neighbours(values, r)
        for t in range(1, tiles - 1):
            here = values[t]
            rows = slice(r * 8, r * 8 + 8)
            cols = slice((t - 1) * 128, t * 128)
            dens_ref[step, rows, cols] = jnp.where(live, here, 0.0)
            wall = edge(t, r)
            pairs = (first_neighbours(slot, t, r), (befores[t], afters[t]), third_neighbours(here, wall, wall))
            for q, (before, after) in enumerate(pairs):
                kicked = vel_ref[q, step, rows, cols] - (after - before) * (REF / 2.0)
                vel_ref[q, step, rows, cols] = jnp.where(live, kicked, 0.0)
    for copy in departures(step):
        copy.start()

    @pl.when(step == slots - 1)
    def _():
        for s in range(PY):
            for copy in departures(s):
                copy.wait()


def relax(flags, patch, density, low, high, velocity):
    slots = density.shape[0]
    rows, cols = interpolation_tables()
    block_rows = jnp.asarray(np.kron(np.eye(slots), rows), jnp.bfloat16)
    table = jnp.asarray(cols, jnp.bfloat16)
    whole = lambda shape: pl.BlockSpec(shape, lambda s, f: (0,) * len(shape), pipeline_mode=pl.Buffered(1))
    return pl.pallas_call(
        relax_kernel,
        grid_spec=pltpu.PrefetchScalarGridSpec(
            num_scalar_prefetch=1,
            grid=(slots,),
            in_specs=[
                whole((slots * 16, 128)),
                whole((slots * 40, slots * 16)),
                whole((128, 2 * LANES)),
                pl.BlockSpec(memory_space=pltpu.HBM),
                pl.BlockSpec(memory_space=pltpu.VMEM),
                pl.BlockSpec(memory_space=pltpu.VMEM),
                pl.BlockSpec(memory_space=pltpu.HBM),
            ],
            out_specs=[pl.BlockSpec(memory_space=pltpu.HBM), pl.BlockSpec(memory_space=pltpu.HBM)],
            scratch_shapes=[
                pltpu.VMEM((slots * 40, 2 * LANES), jnp.float32),
                pltpu.VMEM((2 * (LANES // 128) * ROWS, 128), jnp.float32),
                pltpu.VMEM((LANES // 128, 4, 8, 128), jnp.float32),
                pltpu.VMEM((slots, CELLS, CELLS * CELLS), jnp.float32),
                pltpu.VMEM((3, slots, CELLS, CELLS * CELLS), jnp.float32),
                pltpu.SemaphoreType.DMA((2, slots)),
                pltpu.SemaphoreType.DMA((2, slots)),
            ],
        ),
        out_shape=[
            pltpu.HBM((slots, CELLS, CELLS * CELLS), jnp.float32),
            pltpu.HBM((3, slots, CELLS, CELLS * CELLS), jnp.float32),
        ],
        compiler_params=pltpu.CompilerParams(vmem_limit_bytes=22 << 20),
        name="relax_and_kick",
    )(flags, patch, block_rows, table, in_hbm(density), low, high, in_hbm(velocity))


def local(root_density, subgrid_density, velocity, slot_anchor, slot_count, neighbour):
    place_first = lax.axis_index("px")
    place_second = lax.axis_index("py")
    device = place_first * PY + place_second
    slots = subgrid_density.shape[0]
    q, eig = fourier_basis()
    basis = jnp.asarray(q, jnp.float32)
    eigen = jnp.asarray(eig, jnp.float32)
    low = from_behind(subgrid_density[:, :, -EDGE * CELLS:], "py", 1)
    high = from_behind(subgrid_density[:, :, :EDGE * CELLS], "py", -1)

    packed = forward_third(root_density, q)
    packed = packed.reshape(DEV, 1, MODES * YB * XB)
    got = lax.all_to_all(packed, ("px", "py"), 0, 0, tiled=True).reshape(-1, 128)
    own_eig = eigen[jnp.arange(MODES) * DEV + device]
    solved = solve_planes(own_eig, got, q, eig).reshape(DEV, 1, MODES * PLANE)
    back = lax.all_to_all(solved, ("px", "py"), 0, 0, tiled=True).reshape(-1, 128)

    targets = jnp.arange(PY, dtype=jnp.int32)
    wanted = (place_first * PY + targets) * slots + (place_second - targets) % PY
    anchors = slot_anchor[:, wanted]
    third = (anchors[2][:, None] - 1 + jnp.arange(16, dtype=jnp.int32)[None, :]) % NR
    columns = basis[third.reshape(-1)].T
    start_first = jnp.clip(anchors[0] - place_first * XB, 0, XB - REG)
    start_second = jnp.clip(anchors[1] - place_second * YB, 0, YB - REG)
    sending = cut_patches(back, columns, jnp.stack([start_first, start_second]))
    arrived = lax.all_to_all(sending, "py", 0, 0, tiled=True)
    positions = jnp.arange(slots, dtype=jnp.int32)

    coarse_potential = block_of(back, q)

    first_slot = device * slots
    padded = jnp.pad(neighbour, ((0, 0), (slots, slots)), constant_values=-1)
    nearby = lax.dynamic_slice_in_dim(neighbour, first_slot, slots, 1)
    below = lax.dynamic_slice_in_dim(padded, first_slot, slots, 1)
    above = lax.dynamic_slice_in_dim(padded, first_slot + 2 * slots, slots, 1)
    flags = jnp.stack([
        nearby[0] >= 0, nearby[1] >= 0, below[1] >= 0, above[0] >= 0,
        positions < slot_count[device], (place_second + positions) % PY,
    ], axis=1).astype(jnp.int32)
    subgrid_potential, kicked = relax(flags, arrived, subgrid_density, low, high, velocity)
    return coarse_potential, subgrid_potential, kicked


def solution(mesh):
    return jax.shard_map(
        local,
        mesh=mesh,
        in_specs=(
            P("px", "py", None),
            P(("px", "py"), None, None),
            P(None, ("px", "py"), None, None),
            P(),
            P(),
            P(),
        ),
        out_specs=(
            P("px", "py", None),
            P(("px", "py"), None, None),
            P(None, ("px", "py"), None, None),
        ),
        check_vma=False,
    )
```

```python
import ml_dtypes
import numpy as np
import jax
import jax.numpy as jnp
from jax import lax
from jax.experimental import pallas as pl
from jax.experimental.pallas import tpu as pltpu
from jax.sharding import PartitionSpec as P

NR = 384
REG = 8
REF = 4
SWEEPS = 4
CELLS = REG * REF
PX = 8
PY = 16
DEV = PX * PY
MODES = NR // DEV
XB = NR // PX
YB = NR // PY
XE = XB + 2
YE = YB + 4
PLANE = 1408
ROWS = 48
GROUP = 4
TILES_IN = XB * YB // 128
TILES_OUT = PLANE // 128
EDGE = 4
LANES = (CELLS + 2 * EDGE) * CELLS
RELAX = 6.0 / 7.0
HIGH = lax.Precision.HIGH


def fourier_basis():
    n = np.arange(NR)
    k = np.concatenate([[0, NR // 2], np.repeat(np.arange(1, NR // 2), 2)])
    phase = 2.0 * np.pi * ((n[:, None] * k[None, :]) % NR) / NR
    odd = np.zeros(NR, bool)
    odd[3::2] = True
    q = np.where(odd[None, :], np.sin(phase), np.cos(phase)) * np.sqrt(2.0 / NR)
    q[:, :2] *= np.sqrt(0.5)
    eig = -4.0 * np.sin(np.pi * k / NR) ** 2
    return q, eig


def line_weights(first, last, offset):
    cells = np.arange(first, last)
    marks = 2 * cells + 1 - REF
    low = marks // (2 * REF)
    frac = (marks - 2 * REF * low) / (2.0 * REF)
    table = np.zeros((len(cells), 16))
    rows = np.arange(len(cells))
    table[rows, low + offset] += 1.0 - frac
    table[rows, low + 1 + offset] += frac
    return table


def interpolation_tables():
    wi = line_weights(0, CELLS, 1)[:, :10]
    wlow = line_weights(-1, 0, 1)[:, :10]
    whigh = line_weights(CELLS, CELLS + 1, 1)[:, :10]
    wj = line_weights(-EDGE, CELLS + EDGE, 2)[:, :12]
    jlow = line_weights(-EDGE - 1, -EDGE, 2)[0, :12]
    jhigh = line_weights(CELLS + EDGE, CELLS + EDGE + 1, 2)[0, :12]
    inner = np.einsum("jb,kc->bcjk", wj, wi)
    edge = np.zeros_like(inner)
    edge[:, :, :, 0] += np.einsum("jb,c->bcj", wj, wlow[0])
    edge[:, :, :, -1] += np.einsum("jb,c->bcj", wj, whigh[0])
    edge[:, :, 0, :] += np.einsum("b,kc->bck", jlow, wi)
    edge[:, :, -1, :] += np.einsum("b,kc->bck", jhigh, wi)
    cols = np.zeros((128, 2 * LANES))
    cols[:120, :LANES] = inner.reshape(120, LANES)
    cols[:120, LANES:] = edge.reshape(120, LANES)
    rows = np.zeros((40, 16))
    rows[:32, :10] = wi
    rows[32, :10] = wlow[0]
    rows[33, :10] = whigh[0]
    return rows, cols


def from_behind(value, axis, steps):
    count = lax.axis_size(axis)
    initial, last = (max(0, -steps), min(count, count - steps))
    return lax.ppermute(value, axis, [(source, source + steps) for source in range(initial, last)])


def in_hbm(x):
    return pltpu.with_memory_space_constraint(x, pltpu.HBM)


def in_vmem(x):
    return pltpu.with_memory_space_constraint(x, pltpu.VMEM)


def split3(x):
    hi = x.astype(jnp.bfloat16)
    rest = x - hi.astype(jnp.float32)
    mid = rest.astype(jnp.bfloat16)
    low = (rest - mid.astype(jnp.float32)).astype(jnp.bfloat16)
    return hi, mid, low


def dot(a, b):
    return jnp.dot(a, b, preferred_element_type=jnp.float32)


def split2(x):
    hi = x.astype(jnp.bfloat16)
    return hi, (x - hi.astype(jnp.float32)).astype(jnp.bfloat16)


def table_pair(table):
    hi = np.asarray(table, np.float32).astype(ml_dtypes.bfloat16)
    low = (np.asarray(table) - hi.astype(np.float64)).astype(ml_dtypes.bfloat16)
    return jnp.asarray(np.stack([hi, low]))


def right_product(x, pair):
    hi, low = split2(x)
    return dot(hi, pair[0]) + dot(low, pair[0]) + dot(hi, pair[1])


def left_product(pair, x):
    hi, low = split2(x)
    return dot(pair[0], hi) + dot(pair[0], low) + dot(pair[1], hi)


def moved(tiles, source, target, width, lane, out):
    shift = (target - source) % 128
    rolled = {}
    begin = 0
    while begin < width:
        src, dst = source + begin, target + begin
        end = min(width, begin + 128 - src % 128, begin + 128 - dst % 128)
        if src // 128 not in rolled:
            tile = tiles(src // 128)
            rolled[src // 128] = pltpu.roll(tile, shift, 1) if shift else tile
        tile = rolled[src // 128]
        first, last = dst % 128, dst % 128 + end - begin
        old = out[dst // 128]
        if old is None or first == 0:
            out[dst // 128] = tile
        else:
            out[dst // 128] = jnp.where(lane >= first, tile, old)
        begin = end


def forward_kernel(in_ref, q_hbm, out_ref, rows_ref, q_ref, sem):
    copies = [pltpu.make_async_copy(in_ref.at[:, y], rows_ref.at[y], sem.at[y]) for y in range(YB)]
    table = pltpu.make_async_copy(q_hbm, q_ref, sem.at[YB])
    table.start()
    for copy in copies:
        copy.start()
    table.wait()
    contract = (((1,), (1,)), ((), ()))
    for part in range(3):
        for copy in copies[part * 8:(part + 1) * 8]:
            copy.wait()
        hi, low = split2(rows_ref[part * 8:(part + 1) * 8].reshape(8 * XB, NR))
        modes = None
        for left, right in ((q_ref[0], hi), (q_ref[0], low), (q_ref[1], hi)):
            term = lax.dot_general(left, right, contract, preferred_element_type=jnp.float32)
            modes = term if modes is None else modes + term
        for m in range(MODES):
            for c in range(3):
                out_ref[pl.ds(m * TILES_IN + part * 3 + c, DEV, stride=MODES * TILES_IN), :] = (
                    modes[m * DEV:(m + 1) * DEV, c * 128:(c + 1) * 128])


def forward_third(density, q):
    return pl.pallas_call(
        forward_kernel,
        out_shape=pltpu.HBM((DEV * MODES * TILES_IN, 128), jnp.float32),
        in_specs=[pl.BlockSpec(memory_space=pltpu.HBM), pl.BlockSpec(memory_space=pltpu.HBM)],
        out_specs=pl.BlockSpec(memory_space=pltpu.VMEM),
        scratch_shapes=[pltpu.VMEM((YB, XB, NR), jnp.float32), pltpu.VMEM((2, NR, NR), jnp.bfloat16),
                        pltpu.SemaphoreType.DMA((YB + 1,))],
        compiler_params=pltpu.CompilerParams(vmem_limit_bytes=16 << 20),
        name="forward_third",
    )(in_hbm(density), in_hbm(table_pair(q.T)))


def plane_kernel(mode_ref, in_ref, ax_ref, ay_ref, by_ref, bx_ref, ey_ref, ex_ref, out_ref, x_ref, o_ref):
    lane = lax.broadcasted_iota(jnp.int32, (8, 128), 1)
    stride_in = MODES * TILES_IN
    stride_out = MODES * TILES_OUT
    for m in range(MODES):
        for y in range(YB):
            for h in range(2):
                even, odd = [None, None], [None, None]
                for p in range(PX // 2):
                    loaded = {}

                    def pair(c):
                        if c not in loaded:
                            near = in_ref[pl.ds((p * PY + h * 8) * stride_in + m * TILES_IN + c, 8, stride=stride_in), :]
                            far = in_ref[pl.ds(((p + PX // 2) * PY + h * 8) * stride_in + m * TILES_IN + c, 8,
                                               stride=stride_in), :]
                            loaded[c] = (near + far, near - far)
                        return loaded[c]

                    moved(lambda c: pair(c)[0], y * XB, p * XB, XB, lane, even)
                    moved(lambda c: pair(c)[1], y * XB, p * XB, XB, lane, odd)
                row = y * PY + h * 8
                for t, tile in enumerate(even + odd):
                    x_ref[m, row:row + 8, t * 128:(t + 1) * 128] = tile
    second = [jnp.broadcast_to(ey_ref[i:i + 1, :], (128, 256)).T[:NR // 2, :1] for i in range(2)]
    for m in range(MODES):
        z = jnp.concatenate([right_product(x_ref[m, :, i * 256:i * 256 + NR // 2], ax_ref.at[i]) for i in range(2)], axis=1)
        z = z.reshape(YB, PY, 512)
        near = z[:, :8].reshape(YB * 8, 512)
        far = z[:, 8:].reshape(YB * 8, 512)
        halves = []
        for i, z in enumerate((near + far, near - far)):
            z = left_product(ay_ref.at[i], z)
            total = mode_ref[m] + second[i] + ex_ref[...]
            is_zero = total == 0.0
            z = jnp.where(is_zero, 0.0, z / jnp.where(is_zero, -1.0, total))
            halves.append(left_product(by_ref.at[i], z))
        z = jnp.concatenate([halves[0] + halves[1], halves[0] - halves[1]], axis=0)
        even, odd = (right_product(z[:, i * 256:i * 256 + NR // 2], bx_ref.at[i]) for i in range(2))
        o_ref[m, :, :256] = even + odd
        o_ref[m, :, 256:] = even - odd
    for m in range(MODES):
        for p in range(PX):
            for h in range(2):
                out = [None] * TILES_OUT
                for y in range(YE):
                    row = h * YE * 8 + y * 8
                    moved(lambda t: o_ref[m, row:row + 8, t * 128:(t + 1) * 128], p * 64, y * XE, XE, lane, out)
                for t in range(TILES_OUT):
                    out_ref[pl.ds((p * PY + h * 8) * stride_out + m * TILES_OUT + t, 8, stride=stride_out), :] = out[t]


def solve_planes(own_eig, got, q, eig):
    k = np.rint(np.arcsin(np.sqrt(-eig / 4.0)) * NR / np.pi).astype(int)
    n = np.arange(NR // 2)
    order = (n % 8) * YB + n // 8
    wide = ((np.arange(YE)[:, None] - 2 + np.arange(8)[None, :] * YB) % NR).reshape(-1)
    half = NR // 2
    tables = [[], [], [], []]
    ey = np.zeros((2, 256))
    ex = np.full((1, 512), -1.0)
    for i in range(2):
        part = q[:, k % 2 == i]
        ey[i, :half] = eig[k % 2 == i]
        ex[0, i * 256:i * 256 + half] = eig[k % 2 == i]
        ax = np.zeros((half, 256))
        ax[:half, :half] = part[:half]
        bx = np.zeros((half, PX // 2, 64))
        for p in range(PX // 2):
            bx[:half, p, :XE] = part[(p * XB + np.arange(XE) - 1) % NR].T
        for bucket, table in zip(tables, (ax, part[order].T, part[wide], bx.reshape(half, 256))):
            bucket.append(table_pair(table))
    tables = [jnp.stack(bucket) for bucket in tables]
    vmem = pl.BlockSpec(memory_space=pltpu.VMEM)
    return pl.pallas_call(
        plane_kernel,
        out_shape=pltpu.HBM((DEV * MODES * TILES_OUT, 128), jnp.float32),
        in_specs=[pl.BlockSpec(memory_space=pltpu.SMEM)] + [vmem] * 7,
        out_specs=vmem,
        scratch_shapes=[pltpu.VMEM((MODES, NR, 512), jnp.float32), pltpu.VMEM((MODES, YE * PY, 512), jnp.float32)],
        compiler_params=pltpu.CompilerParams(vmem_limit_bytes=20 << 20),
        name="solve_planes",
    )(own_eig, in_vmem(got), *tables, jnp.asarray(ey, jnp.float32), jnp.asarray(ex, jnp.float32))


def columns_of(s_ref, pair):
    total = None
    for m in range(MODES):
        rows = jnp.concatenate(
            [s_ref[pl.ds(m * TILES_OUT + c, DEV, stride=MODES * TILES_OUT), :] for c in range(TILES_OUT)], axis=1)
        hi, low = split2(rows)
        rows = slice(m * DEV, (m + 1) * DEV)
        for left, right in ((hi, pair[0, rows]), (low, pair[0, rows]), (hi, pair[1, rows])):
            part = lax.dot_general(left, right, (((0,), (0,)), ((), ())), preferred_element_type=jnp.float32)
            total = part if total is None else total + part
    return total


def cut_kernel(start_ref, s_ref, g_ref, out_ref, p_ref):
    cells = columns_of(s_ref, jnp.stack(split2(g_ref[...])))
    for y in range(YE):
        p_ref[y, :XE, :] = cells[y * XE:(y + 1) * XE, :]
    lane = lax.broadcasted_iota(jnp.int32, (16, 128), 1)
    inside = lax.broadcasted_iota(jnp.int32, (16, 128), 0) < REG + 2
    for t in range(PY):
        acc = jnp.zeros((16, 128), jnp.float32)
        for b in range(12):
            first = pl.multiple_of(start_ref[0, t], 8)
            tile = p_ref[start_ref[1, t] + b, pl.ds(first, 16), (t // 8) * 128:(t // 8 + 1) * 128]
            shift = (b * 10 - (t % 8) * 16) % 128
            if shift:
                tile = pltpu.roll(tile, shift, 1)
            acc = jnp.where((lane >= b * 10) & (lane < b * 10 + 10) & inside, tile, acc)
        out_ref[t * 16:(t + 1) * 16, :] = acc


def cut_patches(spectrum, columns, starts):
    return pl.pallas_call(
        cut_kernel,
        out_shape=jax.ShapeDtypeStruct((PY * 16, 128), jnp.float32),
        in_specs=[pl.BlockSpec(memory_space=pltpu.SMEM),
                  pl.BlockSpec(memory_space=pltpu.VMEM),
                  pl.BlockSpec(memory_space=pltpu.VMEM)],
        out_specs=pl.BlockSpec(memory_space=pltpu.VMEM),
        scratch_shapes=[pltpu.VMEM((YE, 56, 256), jnp.float32)],
        compiler_params=pltpu.CompilerParams(vmem_limit_bytes=12 << 20),
        name="cut_patches",
    )(starts, spectrum, columns)


def block_kernel(s_ref, q_hbm, out_ref, q_ref, sem):
    copy = pltpu.make_async_copy(q_hbm, q_ref, sem)
    copy.start()
    copy.wait()
    cells = columns_of(s_ref, q_ref)
    for y in range(YB):
        first = (y + 2) * XE + 1
        out_ref[:, y, :] = cells[first:first + XB, :]


def block_of(spectrum, q):
    return pl.pallas_call(
        block_kernel,
        out_shape=jax.ShapeDtypeStruct((XB, YB, NR), jnp.float32),
        in_specs=[pl.BlockSpec(memory_space=pltpu.VMEM), pl.BlockSpec(memory_space=pltpu.HBM)],
        out_specs=pl.BlockSpec(memory_space=pltpu.VMEM),
        scratch_shapes=[pltpu.VMEM((2, NR, NR), jnp.bfloat16), pltpu.SemaphoreType.DMA],
        compiler_params=pltpu.CompilerParams(vmem_limit_bytes=14 << 20),
        name="block_of",
    )(spectrum, in_hbm(table_pair(q.T)))


def relax_kernel(flag_ref, patch_ref, rows_ref, cols_ref, dens_hbm, low_ref, high_ref, vel_hbm,
                 pot_hbm, out_hbm, grid_ref, v_ref, f_ref, dens_ref, vel_ref, beside_ref, in_sem, out_sem):
    step = pl.program_id(0)

    def arrivals(s):
        return (pltpu.make_async_copy(dens_hbm.at[s], dens_ref.at[s], in_sem.at[0, s]),
                pltpu.make_async_copy(vel_hbm.at[:, s], vel_ref.at[:, s], in_sem.at[1, s]))

    def departures(s):
        return (pltpu.make_async_copy(dens_ref.at[s], pot_hbm.at[s], out_sem.at[0, s]),
                pltpu.make_async_copy(vel_ref.at[:, s], out_hbm.at[:, s], out_sem.at[1, s]))

    @pl.when(step == 0)
    def _():
        for s in range(PY):
            for copy in arrivals(s):
                copy.start()

    @pl.when(step == 0)
    def _():
        source = lax.broadcasted_iota(jnp.int32, (512, 256), 0) % 256
        target = lax.broadcasted_iota(jnp.int32, (512, 256), 1)
        apart = jnp.abs(source - target)
        near = (apart == CELLS) | ((apart == 1) & (source // CELLS == target // CELLS))
        beside_ref[...] = jnp.where(near, 1.0, 0.0).astype(jnp.bfloat16)
        rows = rows_ref[...]
        ordered = jnp.concatenate(
            [patch_ref[pl.ds(pl.multiple_of(flag_ref[j, 5] * 16, 16), 16), :] for j in range(PY)], axis=0)
        expanded = jnp.zeros((640, 128), jnp.float32)
        for part in split3(ordered):
            expanded += dot(rows, part)
        pair = jnp.concatenate(split2(expanded), axis=1)
        for n in range(0, 2 * LANES, 256):
            table = cols_ref[:, n:n + 256]
            grid_ref[:, n:n + 256] = dot(pair, jnp.concatenate([table, table], axis=0))

    tiles = LANES // 128
    lane = lax.broadcasted_iota(jnp.int32, (8, 128), 1)
    third_first = lane % CELLS == 0
    third_last = lane % CELLS == CELLS - 1
    second_first = lane < CELLS
    second_last = lane >= 128 - CELLS
    zero = jnp.zeros((8, 128), jnp.float32)
    slot_of = [step * GROUP + g for g in range(GROUP)]
    bases = [pl.multiple_of(s * 40, 8) for s in slot_of]
    flag = lambda g, i: jnp.broadcast_to(flag_ref[slot_of[g], i], (8, 128)) > 0
    use_low, use_high, same_low, same_high, live = ([flag(g, i) for g in range(GROUP)] for i in range(5))

    def start(g, t, r):
        return grid_ref[pl.ds(bases[g] + r * 8, 8), t * 128:(t + 1) * 128]

    def edge(g, t, r):
        return grid_ref[pl.ds(bases[g] + r * 8, 8), LANES + t * 128:LANES + (t + 1) * 128]

    def row_of(buffer, g, t, r):
        return ((buffer * GROUP + g) * tiles + t) * ROWS + 8 + r * 8

    def value(buffer, g, t, r):
        row = row_of(buffer, g, t, r)
        return v_ref[row:row + 8, :]

    def first_neighbours(buffer, g, t, r):
        row = row_of(buffer, g, t, r)
        return v_ref[row - 1:row + 7, :], v_ref[row + 1:row + 9, :]

    def prepare(g):
        s = slot_of[g]
        for copy in arrivals(s):
            copy.wait()
        for t in range(tiles):
            faces = grid_ref[pl.ds(bases[g] + 32, 8), t * 128:(t + 1) * 128]
            for buffer in range(2):
                row = row_of(buffer, g, t, 0)
                v_ref[row - 1:row, :] = faces[0:1]
                v_ref[row + CELLS:row + CELLS + 1, :] = faces[1:2]
            for r in range(4):
                rows = slice(r * 8, r * 8 + 8)
                if t == 0:
                    rho = low_ref[s, rows, :]
                elif t == tiles - 1:
                    rho = high_ref[s, rows, :]
                else:
                    rho = dens_ref[s, rows, (t - 1) * 128:t * 128]
                fixed = edge(g, t, r) - rho * (1.0 / (REF * REF))
                if t == 0:
                    fixed -= jnp.where(second_first, pltpu.roll(start(g, tiles - 1, r), CELLS, 1), zero)
                if t == tiles - 1:
                    fixed -= jnp.where(second_last, pltpu.roll(start(g, 0, r), 128 - CELLS, 1), zero)
                f_ref[g, t, r] = fixed
                row = row_of(0, g, t, r)
                v_ref[row:row + 8, :] = start(g, t, r)

    pairs = [(tiles - 1, 0)] + [(t, t + 1) for t in range(1, tiles - 1, 2)]
    beside = beside_ref[...]

    def around_of(buffer, members):
        stacked = jnp.concatenate([
            jnp.concatenate([v_ref[row_of(buffer, g, t, 0):row_of(buffer, g, t, 4), :] for t in pair], axis=1)
            for g in members for pair in pairs
        ], axis=0)
        return dot(jnp.concatenate(split2(stacked), axis=1), beside)

    def update(buffer, members, around):
        for m, g in enumerate(members):
            for p, pair in enumerate(pairs):
                for side, t in enumerate(pair):
                    for r in range(4):
                        here = value(buffer, g, t, r)
                        if side == 0:
                            other = pltpu.roll(value(buffer, g, t - 1, r), CELLS, 1)
                            if t == tiles - 1:
                                other = jnp.where(same_high[g], other, pltpu.roll(start(g, t - 1, r), CELLS, 1))
                            other = jnp.where(second_first, other, zero)
                        else:
                            other = pltpu.roll(value(buffer, g, t + 1, r), 128 - CELLS, 1)
                            if t == 0:
                                other = jnp.where(same_low[g], other, pltpu.roll(start(g, t + 1, r), 128 - CELLS, 1))
                            other = jnp.where(second_last, other, zero)
                        before, after = first_neighbours(buffer, g, t, r)
                        row = (m * len(pairs) + p) * CELLS + r * 8
                        total = (here + f_ref[g, t, r]) + (before + after) + (
                            around[row:row + 8, side * 128:(side + 1) * 128] + other)
                        new = total * (1.0 - RELAX)
                        if t == 0:
                            new = jnp.where(use_low[g], new, here)
                        if t == tiles - 1:
                            new = jnp.where(use_high[g], new, here)
                        row = row_of(1 - buffer, g, t, r)
                        v_ref[row:row + 8, :] = new

    def kick(buffer, g):
        s = slot_of[g]
        for r in range(4):
            values = [value(buffer, g, t, r) for t in range(tiles)]
            up = [pltpu.roll(here, CELLS, 1) for here in values]
            down = [pltpu.roll(here, 128 - CELLS, 1) for here in values]
            for t in range(1, tiles - 1):
                here = values[t]
                rows = slice(r * 8, r * 8 + 8)
                cols = slice((t - 1) * 128, t * 128)
                dens_ref[s, rows, cols] = jnp.where(live[g], here, 0.0)
                wall = edge(g, t, r)
                ends = (
                    first_neighbours(buffer, g, t, r),
                    (jnp.where(second_first, up[t - 1], up[t]), jnp.where(second_last, down[t + 1], down[t])),
                    (jnp.where(third_first, wall, pltpu.roll(here, 1, 1)),
                     jnp.where(third_last, wall, pltpu.roll(here, 127, 1))),
                )
                for q, (before, after) in enumerate(ends):
                    kicked = vel_ref[q, s, rows, cols] - (after - before) * (REF / 2.0)
                    vel_ref[q, s, rows, cols] = jnp.where(live[g], kicked, 0.0)
        for copy in departures(s):
            copy.start()

    halves = [range(0, GROUP // 2), range(GROUP // 2, GROUP)]
    for g in range(GROUP):
        prepare(g)
    for sweep in range(SWEEPS):
        buffer = sweep % 2
        arounds = [around_of(buffer, members) for members in halves]
        for members, around in zip(halves, arounds):
            update(buffer, members, around)
    for g in range(GROUP):
        kick(SWEEPS % 2, g)

    @pl.when(step == pl.num_programs(0) - 1)
    def _():
        for s in range(PY):
            for copy in departures(s):
                copy.wait()


def relax(flags, patch, density, low, high, velocity):
    slots = density.shape[0]
    rows, cols = interpolation_tables()
    block_rows = jnp.asarray(np.kron(np.eye(slots), rows), jnp.bfloat16)
    table = jnp.asarray(cols, jnp.bfloat16)
    whole = lambda shape: pl.BlockSpec(shape, lambda s, f: (0,) * len(shape), pipeline_mode=pl.Buffered(1))
    return pl.pallas_call(
        relax_kernel,
        grid_spec=pltpu.PrefetchScalarGridSpec(
            num_scalar_prefetch=1,
            grid=(slots // GROUP,),
            in_specs=[
                whole((slots * 16, 128)),
                whole((slots * 40, slots * 16)),
                whole((128, 2 * LANES)),
                pl.BlockSpec(memory_space=pltpu.HBM),
                pl.BlockSpec(memory_space=pltpu.VMEM),
                pl.BlockSpec(memory_space=pltpu.VMEM),
                pl.BlockSpec(memory_space=pltpu.HBM),
            ],
            out_specs=[pl.BlockSpec(memory_space=pltpu.HBM), pl.BlockSpec(memory_space=pltpu.HBM)],
            scratch_shapes=[
                pltpu.VMEM((slots * 40, 2 * LANES), jnp.float32),
                pltpu.VMEM((2 * GROUP * (LANES // 128) * ROWS, 128), jnp.float32),
                pltpu.VMEM((GROUP, LANES // 128, 4, 8, 128), jnp.float32),
                pltpu.VMEM((slots, CELLS, CELLS * CELLS), jnp.float32),
                pltpu.VMEM((3, slots, CELLS, CELLS * CELLS), jnp.float32),
                pltpu.VMEM((512, 256), jnp.bfloat16),
                pltpu.SemaphoreType.DMA((2, slots)),
                pltpu.SemaphoreType.DMA((2, slots)),
            ],
        ),
        out_shape=[
            pltpu.HBM((slots, CELLS, CELLS * CELLS), jnp.float32),
            pltpu.HBM((3, slots, CELLS, CELLS * CELLS), jnp.float32),
        ],
        compiler_params=pltpu.CompilerParams(vmem_limit_bytes=26 << 20),
        name="relax_and_kick",
    )(flags, patch, block_rows, table, in_hbm(density), low, high, in_hbm(velocity))


def local(root_density, subgrid_density, velocity, slot_anchor, slot_count, neighbour):
    place_first = lax.axis_index("px")
    place_second = lax.axis_index("py")
    device = place_first * PY + place_second
    slots = subgrid_density.shape[0]
    q, eig = fourier_basis()
    basis = jnp.asarray(q, jnp.float32)
    eigen = jnp.asarray(eig, jnp.float32)
    low = from_behind(subgrid_density[:, :, -EDGE * CELLS:], "py", 1)
    high = from_behind(subgrid_density[:, :, :EDGE * CELLS], "py", -1)

    packed = forward_third(root_density, q)
    packed = packed.reshape(DEV, 1, MODES * YB * XB)
    got = lax.all_to_all(packed, ("px", "py"), 0, 0, tiled=True).reshape(-1, 128)
    own_eig = eigen[jnp.arange(MODES) * DEV + device]
    solved = solve_planes(own_eig, got, q, eig).reshape(DEV, 1, MODES * PLANE)
    back = lax.all_to_all(solved, ("px", "py"), 0, 0, tiled=True).reshape(-1, 128)

    targets = jnp.arange(PY, dtype=jnp.int32)
    wanted = (place_first * PY + targets) * slots + (place_second - targets) % PY
    anchors = slot_anchor[:, wanted]
    third = (anchors[2][:, None] - 1 + jnp.arange(16, dtype=jnp.int32)[None, :]) % NR
    columns = basis[third.reshape(-1)].T
    start_first = jnp.clip(anchors[0] - place_first * XB, 0, XB - REG)
    start_second = jnp.clip(anchors[1] - place_second * YB, 0, YB - REG)
    sending = cut_patches(back, columns, jnp.stack([start_first, start_second]))
    arrived = lax.all_to_all(sending, "py", 0, 0, tiled=True)
    positions = jnp.arange(slots, dtype=jnp.int32)

    coarse_potential = block_of(back, q)

    first_slot = device * slots
    padded = jnp.pad(neighbour, ((0, 0), (slots, slots)), constant_values=-1)
    nearby = lax.dynamic_slice_in_dim(neighbour, first_slot, slots, 1)
    below = lax.dynamic_slice_in_dim(padded, first_slot, slots, 1)
    above = lax.dynamic_slice_in_dim(padded, first_slot + 2 * slots, slots, 1)
    flags = jnp.stack([
        nearby[0] >= 0, nearby[1] >= 0, below[1] >= 0, above[0] >= 0,
        positions < slot_count[device], (place_second + positions) % PY,
    ], axis=1).astype(jnp.int32)
    subgrid_potential, kicked = relax(flags, arrived, subgrid_density, low, high, velocity)
    return coarse_potential, subgrid_potential, kicked


def solution(mesh):
    return jax.shard_map(
        local,
        mesh=mesh,
        in_specs=(
            P("px", "py", None),
            P(("px", "py"), None, None),
            P(None, ("px", "py"), None, None),
            P(),
            P(),
            P(),
        ),
        out_specs=(
            P("px", "py", None),
            P(("px", "py"), None, None),
            P(None, ("px", "py"), None, None),
        ),
        check_vma=False,
    )
```

```python
import ml_dtypes
import numpy as np
import jax
import jax.numpy as jnp
from jax import lax
from jax.experimental import pallas as pl
from jax.experimental.pallas import tpu as pltpu
from jax.sharding import PartitionSpec as P

NR = 384
REG = 8
REF = 4
SWEEPS = 4
CELLS = REG * REF
PX = 8
PY = 16
DEV = PX * PY
MODES = NR // DEV
XB = NR // PX
YB = NR // PY
XE = XB + 2
YE = YB + 4
PLANE = 1408
ROWS = 48
GROUP = 8
TILES_IN = XB * YB // 128
TILES_OUT = PLANE // 128
EDGE = 4
LANES = (CELLS + 2 * EDGE) * CELLS
RELAX = 6.0 / 7.0
HIGH = lax.Precision.HIGH


def fourier_basis():
    n = np.arange(NR)
    k = np.concatenate([[0, NR // 2], np.repeat(np.arange(1, NR // 2), 2)])
    phase = 2.0 * np.pi * ((n[:, None] * k[None, :]) % NR) / NR
    odd = np.zeros(NR, bool)
    odd[3::2] = True
    q = np.where(odd[None, :], np.sin(phase), np.cos(phase)) * np.sqrt(2.0 / NR)
    q[:, :2] *= np.sqrt(0.5)
    eig = -4.0 * np.sin(np.pi * k / NR) ** 2
    return q, eig


def line_weights(first, last, offset):
    cells = np.arange(first, last)
    marks = 2 * cells + 1 - REF
    low = marks // (2 * REF)
    frac = (marks - 2 * REF * low) / (2.0 * REF)
    table = np.zeros((len(cells), 16))
    rows = np.arange(len(cells))
    table[rows, low + offset] += 1.0 - frac
    table[rows, low + 1 + offset] += frac
    return table


def interpolation_tables():
    wi = line_weights(0, CELLS, 1)[:, :10]
    wlow = line_weights(-1, 0, 1)[:, :10]
    whigh = line_weights(CELLS, CELLS + 1, 1)[:, :10]
    wj = line_weights(-EDGE, CELLS + EDGE, 2)[:, :12]
    jlow = line_weights(-EDGE - 1, -EDGE, 2)[0, :12]
    jhigh = line_weights(CELLS + EDGE, CELLS + EDGE + 1, 2)[0, :12]
    inner = np.einsum("jb,kc->bcjk", wj, wi)
    edge = np.zeros_like(inner)
    edge[:, :, :, 0] += np.einsum("jb,c->bcj", wj, wlow[0])
    edge[:, :, :, -1] += np.einsum("jb,c->bcj", wj, whigh[0])
    edge[:, :, 0, :] += np.einsum("b,kc->bck", jlow, wi)
    edge[:, :, -1, :] += np.einsum("b,kc->bck", jhigh, wi)
    cols = np.zeros((128, 2 * LANES))
    cols[:120, :LANES] = inner.reshape(120, LANES)
    cols[:120, LANES:] = edge.reshape(120, LANES)
    rows = np.zeros((40, 16))
    rows[:32, :10] = wi
    rows[32, :10] = wlow[0]
    rows[33, :10] = whigh[0]
    return rows, cols


def from_behind(value, axis, steps):
    count = lax.axis_size(axis)
    initial, last = (max(0, -steps), min(count, count - steps))
    return lax.ppermute(value, axis, [(source, source + steps) for source in range(initial, last)])


def in_hbm(x):
    return pltpu.with_memory_space_constraint(x, pltpu.HBM)


def in_vmem(x):
    return pltpu.with_memory_space_constraint(x, pltpu.VMEM)


def split3(x):
    hi = x.astype(jnp.bfloat16)
    rest = x - hi.astype(jnp.float32)
    mid = rest.astype(jnp.bfloat16)
    low = (rest - mid.astype(jnp.float32)).astype(jnp.bfloat16)
    return hi, mid, low


def dot(a, b):
    return jnp.dot(a, b, preferred_element_type=jnp.float32)


def split2(x):
    hi = x.astype(jnp.bfloat16)
    return hi, (x - hi.astype(jnp.float32)).astype(jnp.bfloat16)


def table_pair(table):
    hi = np.asarray(table, np.float32).astype(ml_dtypes.bfloat16)
    low = (np.asarray(table) - hi.astype(np.float64)).astype(ml_dtypes.bfloat16)
    return jnp.asarray(np.stack([hi, low]))


def padded(x):
    rows = -x.shape[0] % 256
    return jnp.concatenate([x, jnp.zeros((rows, x.shape[1]), x.dtype)], axis=0) if rows else x


def right_product(x, pair):
    hi, low = split2(x)
    first, second = padded(pair[0]), padded(pair[1])
    return dot(jnp.concatenate([hi, low, hi], axis=1), jnp.concatenate([first, first, second], axis=0))


def left_product(pair, x):
    hi, low = (padded(part) for part in split2(x))
    return dot(jnp.concatenate([pair[0], pair[0], pair[1]], axis=1), jnp.concatenate([hi, low, hi], axis=0))


def moved(tiles, source, target, width, lane, out):
    shift = (target - source) % 128
    rolled = {}
    begin = 0
    while begin < width:
        src, dst = source + begin, target + begin
        end = min(width, begin + 128 - src % 128, begin + 128 - dst % 128)
        if src // 128 not in rolled:
            tile = tiles(src // 128)
            rolled[src // 128] = pltpu.roll(tile, shift, 1) if shift else tile
        tile = rolled[src // 128]
        first, last = dst % 128, dst % 128 + end - begin
        old = out[dst // 128]
        if old is None or first == 0:
            out[dst // 128] = tile
        else:
            out[dst // 128] = jnp.where(lane >= first, tile, old)
        begin = end


def forward_kernel(in_ref, q_hbm, out_ref, rows_ref, q_ref, sem):
    copies = [pltpu.make_async_copy(in_ref.at[:, y], rows_ref.at[y], sem.at[y]) for y in range(YB)]
    table = pltpu.make_async_copy(q_hbm, q_ref, sem.at[YB])
    table.start()
    for copy in copies:
        copy.start()
    table.wait()
    contract = (((1,), (1,)), ((), ()))
    for part in range(3):
        for copy in copies[part * 8:(part + 1) * 8]:
            copy.wait()
        hi, low = split2(rows_ref[part * 8:(part + 1) * 8].reshape(8 * XB, NR))
        modes = lax.dot_general(
            jnp.concatenate([q_ref[0], q_ref[0], q_ref[1]], axis=1), jnp.concatenate([hi, low, hi], axis=1),
            contract, preferred_element_type=jnp.float32)
        for m in range(MODES):
            for c in range(3):
                out_ref[pl.ds(m * TILES_IN + part * 3 + c, DEV, stride=MODES * TILES_IN), :] = (
                    modes[m * DEV:(m + 1) * DEV, c * 128:(c + 1) * 128])


def forward_third(density, q):
    return pl.pallas_call(
        forward_kernel,
        out_shape=pltpu.HBM((DEV * MODES * TILES_IN, 128), jnp.float32),
        in_specs=[pl.BlockSpec(memory_space=pltpu.HBM), pl.BlockSpec(memory_space=pltpu.HBM)],
        out_specs=pl.BlockSpec(memory_space=pltpu.VMEM),
        scratch_shapes=[pltpu.VMEM((YB, XB, NR), jnp.float32), pltpu.VMEM((2, NR, NR), jnp.bfloat16),
                        pltpu.SemaphoreType.DMA((YB + 1,))],
        compiler_params=pltpu.CompilerParams(vmem_limit_bytes=16 << 20),
        name="forward_third",
    )(in_hbm(density), in_hbm(table_pair(q.T)))


def plane_kernel(mode_ref, in_ref, ax_ref, ay_ref, by_ref, bx_ref, ey_ref, ex_ref, out_ref, x_ref, o_ref):
    lane = lax.broadcasted_iota(jnp.int32, (8, 128), 1)
    stride_in = MODES * TILES_IN
    stride_out = MODES * TILES_OUT
    second = [jnp.broadcast_to(ey_ref[i:i + 1, :], (128, 256)).T[:NR // 2, :1] for i in range(2)]
    def unpack(m):
        for y in range(YB):
            for h in range(2):
                even, odd = [None, None], [None, None]
                for p in range(PX // 2):
                    loaded = {}

                    def pair(c):
                        if c not in loaded:
                            near = in_ref[pl.ds((p * PY + h * 8) * stride_in + m * TILES_IN + c, 8, stride=stride_in), :]
                            far = in_ref[pl.ds(((p + PX // 2) * PY + h * 8) * stride_in + m * TILES_IN + c, 8,
                                               stride=stride_in), :]
                            loaded[c] = (near + far, near - far)
                        return loaded[c]

                    moved(lambda c: pair(c)[0], y * XB, p * XB, XB, lane, even)
                    moved(lambda c: pair(c)[1], y * XB, p * XB, XB, lane, odd)
                row = y * PY + h * 8
                for t, tile in enumerate(even + odd):
                    x_ref[m, row:row + 8, t * 128:(t + 1) * 128] = tile

    def transform(m):
        z = jnp.concatenate([right_product(x_ref[m, :, i * 256:(i + 1) * 256], ax_ref.at[i]) for i in range(2)], axis=1)
        z = z.reshape(YB, PY, 512)
        near = z[:, :8].reshape(YB * 8, 512)
        far = z[:, 8:].reshape(YB * 8, 512)
        halves = []
        for i, z in enumerate((near + far, near - far)):
            z = left_product(ay_ref.at[i], z)
            total = mode_ref[m] + second[i] + ex_ref[...]
            is_zero = total == 0.0
            z = jnp.where(is_zero, 0.0, z / jnp.where(is_zero, -1.0, total))
            halves.append(left_product(by_ref.at[i], z))
        z = jnp.concatenate([halves[0] + halves[1], halves[0] - halves[1]], axis=0)
        even, odd = (right_product(z[:, i * 256:(i + 1) * 256], bx_ref.at[i]) for i in range(2))
        o_ref[m, :, :256] = even + odd
        o_ref[m, :, 256:] = even - odd

    def pack(m):
        for p in range(PX):
            for h in range(2):
                out = [None] * TILES_OUT
                for y in range(YE):
                    row = h * YE * 8 + y * 8
                    moved(lambda t: o_ref[m, row:row + 8, t * 128:(t + 1) * 128], p * 64, y * XE, XE, lane, out)
                for t in range(TILES_OUT):
                    out_ref[pl.ds((p * PY + h * 8) * stride_out + m * TILES_OUT + t, 8, stride=stride_out), :] = out[t]

    unpack(0)
    transform(0)
    unpack(1)
    transform(1)
    pack(0)
    unpack(2)
    transform(2)
    pack(1)
    pack(2)


def solve_planes(own_eig, got, q, eig):
    k = np.rint(np.arcsin(np.sqrt(-eig / 4.0)) * NR / np.pi).astype(int)
    n = np.arange(NR // 2)
    order = (n % 8) * YB + n // 8
    wide = ((np.arange(YE)[:, None] - 2 + np.arange(8)[None, :] * YB) % NR).reshape(-1)
    half = NR // 2
    tables = [[], [], [], []]
    ey = np.zeros((2, 256))
    ex = np.full((1, 512), -1.0)
    for i in range(2):
        part = q[:, k % 2 == i]
        ey[i, :half] = eig[k % 2 == i]
        ex[0, i * 256:i * 256 + half] = eig[k % 2 == i]
        ax = np.zeros((half, 256))
        ax[:half, :half] = part[:half]
        bx = np.zeros((half, PX // 2, 64))
        for p in range(PX // 2):
            bx[:half, p, :XE] = part[(p * XB + np.arange(XE) - 1) % NR].T
        for bucket, table in zip(tables, (ax, np.pad(part[order].T, ((0, 0), (0, 256 - half))),
                                          np.pad(part[wide], ((0, 0), (0, 256 - half))), bx.reshape(half, 256))):
            bucket.append(table_pair(table))
    tables = [jnp.stack(bucket) for bucket in tables]
    vmem = pl.BlockSpec(memory_space=pltpu.VMEM)
    return pl.pallas_call(
        plane_kernel,
        out_shape=pltpu.HBM((DEV * MODES * TILES_OUT, 128), jnp.float32),
        in_specs=[pl.BlockSpec(memory_space=pltpu.SMEM)] + [vmem] * 7,
        out_specs=vmem,
        scratch_shapes=[pltpu.VMEM((MODES, NR, 512), jnp.float32), pltpu.VMEM((MODES, YE * PY, 512), jnp.float32)],
        compiler_params=pltpu.CompilerParams(vmem_limit_bytes=20 << 20),
        name="solve_planes",
    )(own_eig, in_vmem(got), *tables, jnp.asarray(ey, jnp.float32), jnp.asarray(ex, jnp.float32))


def stacked_parts(s_ref):
    his, lows = [], []
    for m in range(MODES):
        rows = jnp.concatenate(
            [s_ref[pl.ds(m * TILES_OUT + c, DEV, stride=MODES * TILES_OUT), :] for c in range(TILES_OUT)], axis=1)
        hi, low = split2(rows)
        his.append(hi)
        lows.append(low)
    return jnp.concatenate(his + lows + his, axis=0)


def columns_of(stacked, hi, low):
    right = jnp.concatenate([hi, hi, low], axis=0)
    return lax.dot_general(stacked, right, (((0,), (0,)), ((), ())), preferred_element_type=jnp.float32)


def cut_kernel(start_ref, s_ref, g_ref, out_ref, p_ref):
    cells = columns_of(stacked_parts(s_ref), *split2(g_ref[...]))
    for y in range(YE):
        p_ref[y, :XE, :] = cells[y * XE:(y + 1) * XE, :]
    lane = lax.broadcasted_iota(jnp.int32, (16, 128), 1)
    inside = lax.broadcasted_iota(jnp.int32, (16, 128), 0) < REG + 2
    for t in range(PY):
        acc = jnp.zeros((16, 128), jnp.float32)
        for b in range(12):
            first = pl.multiple_of(start_ref[t, 0], 8)
            tile = p_ref[start_ref[t, 1] + b, pl.ds(first, 16), (t // 8) * 128:(t // 8 + 1) * 128]
            shift = (b * 10 - (t % 8) * 16) % 128
            if shift:
                tile = pltpu.roll(tile, shift, 1)
            acc = jnp.where((lane >= b * 10) & (lane < b * 10 + 10) & inside, tile, acc)
        out_ref[t * 16:(t + 1) * 16, :] = acc


def cut_patches(spectrum, columns, starts):
    return pl.pallas_call(
        cut_kernel,
        out_shape=jax.ShapeDtypeStruct((PY * 16, 128), jnp.float32),
        in_specs=[pl.BlockSpec(memory_space=pltpu.SMEM),
                  pl.BlockSpec(memory_space=pltpu.VMEM),
                  pl.BlockSpec(memory_space=pltpu.VMEM)],
        out_specs=pl.BlockSpec(memory_space=pltpu.VMEM),
        scratch_shapes=[pltpu.VMEM((YE, 56, 256), jnp.float32)],
        compiler_params=pltpu.CompilerParams(vmem_limit_bytes=12 << 20),
        name="cut_patches",
    )(starts, spectrum, columns)


def block_kernel(s_ref, q_hbm, out_ref, q_ref, sem):
    copy = pltpu.make_async_copy(q_hbm, q_ref, sem)
    copy.start()
    stacked = stacked_parts(s_ref)
    copy.wait()
    cells = columns_of(stacked, q_ref[0], q_ref[1])
    for y in range(YB):
        first = (y + 2) * XE + 1
        out_ref[:, y, :] = cells[first:first + XB, :]


def block_of(spectrum, q):
    return pl.pallas_call(
        block_kernel,
        out_shape=jax.ShapeDtypeStruct((XB, YB, NR), jnp.float32),
        in_specs=[pl.BlockSpec(memory_space=pltpu.VMEM), pl.BlockSpec(memory_space=pltpu.HBM)],
        out_specs=pl.BlockSpec(memory_space=pltpu.VMEM),
        scratch_shapes=[pltpu.VMEM((2, NR, NR), jnp.bfloat16), pltpu.SemaphoreType.DMA],
        compiler_params=pltpu.CompilerParams(vmem_limit_bytes=14 << 20),
        name="block_of",
    )(spectrum, in_hbm(table_pair(q.T)))


def relax_kernel(flag_ref, patch_ref, rows_ref, cols_ref, dens_hbm, low_ref, high_ref, vel_hbm,
                 pot_hbm, out_hbm, grid_ref, v_ref, f_ref, dens_ref, vel_ref, beside_ref, in_sem, out_sem):
    step = pl.program_id(0)

    def arrivals(s):
        return (pltpu.make_async_copy(dens_hbm.at[s], dens_ref.at[s], in_sem.at[0, s]),
                pltpu.make_async_copy(vel_hbm.at[:, s], vel_ref.at[:, s], in_sem.at[1, s]))

    def departures(s):
        return (pltpu.make_async_copy(dens_ref.at[s], pot_hbm.at[s], out_sem.at[0, s]),
                pltpu.make_async_copy(vel_ref.at[:, s], out_hbm.at[:, s], out_sem.at[1, s]))

    @pl.when(step == 0)
    def _():
        for s in range(PY):
            for copy in arrivals(s):
                copy.start()

    @pl.when(step == 0)
    def _():
        source = lax.broadcasted_iota(jnp.int32, (512, 256), 0) % 256
        target = lax.broadcasted_iota(jnp.int32, (512, 256), 1)
        apart = jnp.abs(source - target)
        near = (apart == CELLS) | ((apart == 1) & (source // CELLS == target // CELLS))
        beside_ref[...] = jnp.where(near, 1.0, 0.0).astype(jnp.bfloat16)
        rows = rows_ref[...]
        ordered = jnp.concatenate(
            [patch_ref[pl.ds(pl.multiple_of(flag_ref[j, 7] * 16, 16), 16), :] for j in range(PY)], axis=0)
        expanded = jnp.zeros((640, 128), jnp.float32)
        for part in split3(ordered):
            expanded += dot(rows, part)
        pair = jnp.concatenate(split2(expanded), axis=1)
        for n in range(0, 2 * LANES, 256):
            table = cols_ref[:, n:n + 256]
            grid_ref[:, n:n + 256] = dot(pair, jnp.concatenate([table, table], axis=0))

    tiles = LANES // 128
    lane = lax.broadcasted_iota(jnp.int32, (8, 128), 1)
    third_first = lane % CELLS == 0
    third_last = lane % CELLS == CELLS - 1
    second_first = lane < CELLS
    second_last = lane >= 128 - CELLS
    zero = jnp.zeros((8, 128), jnp.float32)
    slot_of = [step * GROUP + g for g in range(GROUP)]
    bases = [pl.multiple_of(s * 40, 8) for s in slot_of]
    flag = lambda g, i: jnp.broadcast_to(flag_ref[slot_of[g], i + 2], (8, 128)) > 0
    use_low, use_high, same_low, same_high, live = ([flag(g, i) for g in range(GROUP)] for i in range(5))

    def start(g, t, r):
        return grid_ref[pl.ds(bases[g] + r * 8, 8), t * 128:(t + 1) * 128]

    def edge(g, t, r):
        return grid_ref[pl.ds(bases[g] + r * 8, 8), LANES + t * 128:LANES + (t + 1) * 128]

    def row_of(buffer, g, t, r):
        return ((buffer * GROUP + g) * tiles + t) * ROWS + 8 + r * 8

    def value(buffer, g, t, r):
        row = row_of(buffer, g, t, r)
        return v_ref[row:row + 8, :]

    def first_neighbours(buffer, g, t, r):
        row = row_of(buffer, g, t, r)
        return v_ref[row - 1:row + 7, :], v_ref[row + 1:row + 9, :]

    def prepare(g):
        s = slot_of[g]
        for copy in arrivals(s):
            copy.wait()
        for t in range(tiles):
            faces = grid_ref[pl.ds(bases[g] + 32, 8), t * 128:(t + 1) * 128]
            for buffer in range(2):
                row = row_of(buffer, g, t, 0)
                v_ref[row - 1:row, :] = faces[0:1]
                v_ref[row + CELLS:row + CELLS + 1, :] = faces[1:2]
            for r in range(4):
                rows = slice(r * 8, r * 8 + 8)
                if t == 0:
                    rho = low_ref[s, rows, :]
                elif t == tiles - 1:
                    rho = high_ref[s, rows, :]
                else:
                    rho = dens_ref[s, rows, (t - 1) * 128:t * 128]
                fixed = edge(g, t, r) - rho * (1.0 / (REF * REF))
                if t == 0:
                    fixed -= jnp.where(second_first, pltpu.roll(start(g, tiles - 1, r), CELLS, 1), zero)
                if t == tiles - 1:
                    fixed -= jnp.where(second_last, pltpu.roll(start(g, 0, r), 128 - CELLS, 1), zero)
                f_ref[g, t, r] = fixed
                row = row_of(0, g, t, r)
                v_ref[row:row + 8, :] = start(g, t, r)

    pairs = [(tiles - 1, 0)] + [(t, t + 1) for t in range(1, tiles - 1, 2)]
    beside = beside_ref[...]

    def around_of(buffer, members):
        stacked = jnp.concatenate([
            jnp.concatenate([v_ref[row_of(buffer, g, t, 0):row_of(buffer, g, t, 4), :] for t in pair], axis=1)
            for g in members for pair in pairs
        ], axis=0)
        return dot(jnp.concatenate(split2(stacked), axis=1), beside)

    def update(buffer, members, around):
        for m, g in enumerate(members):
            for p, pair in enumerate(pairs):
                for side, t in enumerate(pair):
                    for r in range(4):
                        here = value(buffer, g, t, r)
                        if side == 0:
                            other = pltpu.roll(value(buffer, g, t - 1, r), CELLS, 1)
                            if t == tiles - 1:
                                other = jnp.where(same_high[g], other, pltpu.roll(start(g, t - 1, r), CELLS, 1))
                            other = jnp.where(second_first, other, zero)
                        else:
                            other = pltpu.roll(value(buffer, g, t + 1, r), 128 - CELLS, 1)
                            if t == 0:
                                other = jnp.where(same_low[g], other, pltpu.roll(start(g, t + 1, r), 128 - CELLS, 1))
                            other = jnp.where(second_last, other, zero)
                        before, after = first_neighbours(buffer, g, t, r)
                        row = (m * len(pairs) + p) * CELLS + r * 8
                        total = (here + f_ref[g, t, r]) + (before + after) + (
                            around[row:row + 8, side * 128:(side + 1) * 128] + other)
                        new = total * (1.0 - RELAX)
                        if t == 0:
                            new = jnp.where(use_low[g], new, here)
                        if t == tiles - 1:
                            new = jnp.where(use_high[g], new, here)
                        row = row_of(1 - buffer, g, t, r)
                        v_ref[row:row + 8, :] = new

    def kick(buffer, g):
        s = slot_of[g]
        for r in range(4):
            values = [value(buffer, g, t, r) for t in range(tiles)]
            up = [pltpu.roll(here, CELLS, 1) for here in values]
            down = [pltpu.roll(here, 128 - CELLS, 1) for here in values]
            for t in range(1, tiles - 1):
                here = values[t]
                rows = slice(r * 8, r * 8 + 8)
                cols = slice((t - 1) * 128, t * 128)
                dens_ref[s, rows, cols] = jnp.where(live[g], here, 0.0)
                wall = edge(g, t, r)
                ends = (
                    first_neighbours(buffer, g, t, r),
                    (jnp.where(second_first, up[t - 1], up[t]), jnp.where(second_last, down[t + 1], down[t])),
                    (jnp.where(third_first, wall, pltpu.roll(here, 1, 1)),
                     jnp.where(third_last, wall, pltpu.roll(here, 127, 1))),
                )
                for q, (before, after) in enumerate(ends):
                    kicked = vel_ref[q, s, rows, cols] - (after - before) * (REF / 2.0)
                    vel_ref[q, s, rows, cols] = jnp.where(live[g], kicked, 0.0)
        for copy in departures(s):
            copy.start()

    halves = [range(0, GROUP // 2), range(GROUP // 2, GROUP)]
    for g in range(GROUP):
        prepare(g)
    for sweep in range(SWEEPS):
        buffer = sweep % 2
        arounds = [around_of(buffer, members) for members in halves]
        for members, around in zip(halves, arounds):
            update(buffer, members, around)
    for g in range(GROUP):
        kick(SWEEPS % 2, g)

    @pl.when(step == pl.num_programs(0) - 1)
    def _():
        for s in range(PY):
            for copy in departures(s):
                copy.wait()


def relax(flags, patch, density, low, high, velocity):
    slots = density.shape[0]
    rows, cols = interpolation_tables()
    block_rows = jnp.asarray(np.kron(np.eye(slots), rows), jnp.bfloat16)
    table = jnp.asarray(cols, jnp.bfloat16)
    whole = lambda shape: pl.BlockSpec(shape, lambda s, f: (0,) * len(shape), pipeline_mode=pl.Buffered(1))
    return pl.pallas_call(
        relax_kernel,
        grid_spec=pltpu.PrefetchScalarGridSpec(
            num_scalar_prefetch=1,
            grid=(slots // GROUP,),
            in_specs=[
                whole((slots * 16, 128)),
                whole((slots * 40, slots * 16)),
                whole((128, 2 * LANES)),
                pl.BlockSpec(memory_space=pltpu.HBM),
                pl.BlockSpec(memory_space=pltpu.VMEM),
                pl.BlockSpec(memory_space=pltpu.VMEM),
                pl.BlockSpec(memory_space=pltpu.HBM),
            ],
            out_specs=[pl.BlockSpec(memory_space=pltpu.HBM), pl.BlockSpec(memory_space=pltpu.HBM)],
            scratch_shapes=[
                pltpu.VMEM((slots * 40, 2 * LANES), jnp.float32),
                pltpu.VMEM((2 * GROUP * (LANES // 128) * ROWS, 128), jnp.float32),
                pltpu.VMEM((GROUP, LANES // 128, 4, 8, 128), jnp.float32),
                pltpu.VMEM((slots, CELLS, CELLS * CELLS), jnp.float32),
                pltpu.VMEM((3, slots, CELLS, CELLS * CELLS), jnp.float32),
                pltpu.VMEM((512, 256), jnp.bfloat16),
                pltpu.SemaphoreType.DMA((2, slots)),
                pltpu.SemaphoreType.DMA((2, slots)),
            ],
        ),
        out_shape=[
            pltpu.HBM((slots, CELLS, CELLS * CELLS), jnp.float32),
            pltpu.HBM((3, slots, CELLS, CELLS * CELLS), jnp.float32),
        ],
        compiler_params=pltpu.CompilerParams(vmem_limit_bytes=34 << 20),
        name="relax_and_kick",
    )(flags, patch, block_rows, table, in_hbm(density), low, high, in_hbm(velocity))


def local(root_density, subgrid_density, velocity, slot_anchor, slot_count, neighbour):
    place_first = lax.axis_index("px")
    place_second = lax.axis_index("py")
    device = place_first * PY + place_second
    slots = subgrid_density.shape[0]
    q, eig = fourier_basis()
    basis = jnp.asarray(q, jnp.float32)
    eigen = jnp.asarray(eig, jnp.float32)
    low = from_behind(subgrid_density[:, :, -EDGE * CELLS:], "py", 1)
    high = from_behind(subgrid_density[:, :, :EDGE * CELLS], "py", -1)

    packed = forward_third(root_density, q)
    packed = packed.reshape(DEV, 1, MODES * YB * XB)
    got = lax.all_to_all(packed, ("px", "py"), 0, 0, tiled=True).reshape(-1, 128)
    own_eig = eigen[jnp.arange(MODES) * DEV + device]
    solved = solve_planes(own_eig, got, q, eig).reshape(DEV, 1, MODES * PLANE)
    back = lax.all_to_all(solved, ("px", "py"), 0, 0, tiled=True).reshape(-1, 128)

    targets = jnp.arange(PY, dtype=jnp.int32)
    wanted = (place_first * PY + targets) * slots + (place_second - targets) % PY
    anchors = slot_anchor[:, wanted]
    third = (anchors[2][:, None] - 1 + jnp.arange(16, dtype=jnp.int32)[None, :]) % NR
    columns = basis[third.reshape(-1)].T
    start_first = jnp.clip(anchors[0] - place_first * XB, 0, XB - REG)
    start_second = jnp.clip(anchors[1] - place_second * YB, 0, YB - REG)
    positions = jnp.arange(slots, dtype=jnp.int32)
    first_slot = device * slots
    padded = jnp.pad(neighbour, ((0, 0), (slots, slots)), constant_values=-1)
    nearby = lax.dynamic_slice_in_dim(neighbour, first_slot, slots, 1)
    below = lax.dynamic_slice_in_dim(padded, first_slot, slots, 1)
    above = lax.dynamic_slice_in_dim(padded, first_slot + 2 * slots, slots, 1)
    flags = jnp.stack([
        start_first, start_second,
        nearby[0] >= 0, nearby[1] >= 0, below[1] >= 0, above[0] >= 0,
        positions < slot_count[device], (place_second + positions) % PY,
    ], axis=1).astype(jnp.int32)
    sending = cut_patches(back, columns, flags)
    arrived = lax.all_to_all(sending, "py", 0, 0, tiled=True)

    coarse_potential = block_of(back, q)

    subgrid_potential, kicked = relax(flags, arrived, subgrid_density, low, high, velocity)
    return coarse_potential, subgrid_potential, kicked


def solution(mesh):
    return jax.shard_map(
        local,
        mesh=mesh,
        in_specs=(
            P("px", "py", None),
            P(("px", "py"), None, None),
            P(None, ("px", "py"), None, None),
            P(),
            P(),
            P(),
        ),
        out_specs=(
            P("px", "py", None),
            P(("px", "py"), None, None),
            P(None, ("px", "py"), None, None),
        ),
        check_vma=False,
    )
```

```python
import ml_dtypes
import numpy as np
import jax
import jax.numpy as jnp
from jax import lax
from jax.experimental import pallas as pl
from jax.experimental.pallas import tpu as pltpu
from jax.sharding import PartitionSpec as P

NR = 384
REG = 8
REF = 4
SWEEPS = 4
CELLS = REG * REF
PX = 8
PY = 16
DEV = PX * PY
MODES = NR // DEV
XB = NR // PX
YB = NR // PY
XE = XB + 2
YE = YB + 4
PLANE = 1408
ROWS = 48
GROUP = 8
TILES_IN = XB * YB // 128
TILES_OUT = PLANE // 128
EDGE = 4
LANES = (CELLS + 2 * EDGE) * CELLS
RELAX = 6.0 / 7.0
HIGH = lax.Precision.HIGH


def fourier_basis():
    n = np.arange(NR)
    k = np.concatenate([[0, NR // 2], np.repeat(np.arange(1, NR // 2), 2)])
    phase = 2.0 * np.pi * ((n[:, None] * k[None, :]) % NR) / NR
    odd = np.zeros(NR, bool)
    odd[3::2] = True
    q = np.where(odd[None, :], np.sin(phase), np.cos(phase)) * np.sqrt(2.0 / NR)
    q[:, :2] *= np.sqrt(0.5)
    eig = -4.0 * np.sin(np.pi * k / NR) ** 2
    return q, eig


def line_weights(first, last, offset):
    cells = np.arange(first, last)
    marks = 2 * cells + 1 - REF
    low = marks // (2 * REF)
    frac = (marks - 2 * REF * low) / (2.0 * REF)
    table = np.zeros((len(cells), 16))
    rows = np.arange(len(cells))
    table[rows, low + offset] += 1.0 - frac
    table[rows, low + 1 + offset] += frac
    return table


def interpolation_tables():
    wi = line_weights(0, CELLS, 1)[:, :10]
    wlow = line_weights(-1, 0, 1)[:, :10]
    whigh = line_weights(CELLS, CELLS + 1, 1)[:, :10]
    wj = line_weights(-EDGE, CELLS + EDGE, 2)[:, :12]
    jlow = line_weights(-EDGE - 1, -EDGE, 2)[0, :12]
    jhigh = line_weights(CELLS + EDGE, CELLS + EDGE + 1, 2)[0, :12]
    inner = np.einsum("jb,kc->bcjk", wj, wi)
    edge = np.zeros_like(inner)
    edge[:, :, :, 0] += np.einsum("jb,c->bcj", wj, wlow[0])
    edge[:, :, :, -1] += np.einsum("jb,c->bcj", wj, whigh[0])
    edge[:, :, 0, :] += np.einsum("b,kc->bck", jlow, wi)
    edge[:, :, -1, :] += np.einsum("b,kc->bck", jhigh, wi)
    cols = np.zeros((128, 2 * LANES))
    cols[:120, :LANES] = inner.reshape(120, LANES)
    cols[:120, LANES:] = edge.reshape(120, LANES)
    rows = np.zeros((40, 16))
    rows[:32, :10] = wi
    rows[32, :10] = wlow[0]
    rows[33, :10] = whigh[0]
    return rows, cols


def from_behind(value, axis, steps):
    count = lax.axis_size(axis)
    initial, last = (max(0, -steps), min(count, count - steps))
    return lax.ppermute(value, axis, [(source, source + steps) for source in range(initial, last)])


def in_hbm(x):
    return pltpu.with_memory_space_constraint(x, pltpu.HBM)


def in_vmem(x):
    return pltpu.with_memory_space_constraint(x, pltpu.VMEM)


def split3(x):
    hi = x.astype(jnp.bfloat16)
    rest = x - hi.astype(jnp.float32)
    mid = rest.astype(jnp.bfloat16)
    low = (rest - mid.astype(jnp.float32)).astype(jnp.bfloat16)
    return hi, mid, low


def dot(a, b):
    return jnp.dot(a, b, preferred_element_type=jnp.float32)


def split2(x):
    hi = x.astype(jnp.bfloat16)
    return hi, (x - hi.astype(jnp.float32)).astype(jnp.bfloat16)


def table_pair(table):
    hi = np.asarray(table, np.float32).astype(ml_dtypes.bfloat16)
    low = (np.asarray(table) - hi.astype(np.float64)).astype(ml_dtypes.bfloat16)
    return jnp.asarray(np.stack([hi, low]))


def padded(x):
    rows = -x.shape[0] % 256
    return jnp.concatenate([x, jnp.zeros((rows, x.shape[1]), x.dtype)], axis=0) if rows else x


def right_product(x, pair):
    hi, low = split2(x)
    first, second = padded(pair[0]), padded(pair[1])
    return dot(jnp.concatenate([hi, low, hi], axis=1), jnp.concatenate([first, first, second], axis=0))


def left_product(pair, x):
    hi, low = (padded(part) for part in split2(x))
    return dot(jnp.concatenate([pair[0], pair[0], pair[1]], axis=1), jnp.concatenate([hi, low, hi], axis=0))


def moved(tiles, source, target, width, lane, out):
    shift = (target - source) % 128
    rolled = {}
    begin = 0
    while begin < width:
        src, dst = source + begin, target + begin
        end = min(width, begin + 128 - src % 128, begin + 128 - dst % 128)
        if src // 128 not in rolled:
            tile = tiles(src // 128)
            rolled[src // 128] = pltpu.roll(tile, shift, 1) if shift else tile
        tile = rolled[src // 128]
        first, last = dst % 128, dst % 128 + end - begin
        old = out[dst // 128]
        if old is None or first == 0:
            out[dst // 128] = tile
        else:
            out[dst // 128] = jnp.where(lane >= first, tile, old)
        begin = end


def forward_kernel(in_ref, q_hbm, out_ref, rows_ref, q_ref, sem):
    copies = [pltpu.make_async_copy(in_ref.at[:, y], rows_ref.at[y], sem.at[y]) for y in range(YB)]
    table = pltpu.make_async_copy(q_hbm, q_ref, sem.at[YB])
    for copy in copies[:8]:
        copy.start()
    table.start()
    for copy in copies[8:]:
        copy.start()
    table.wait()
    contract = (((1,), (1,)), ((), ()))
    for part in range(3):
        for copy in copies[part * 8:(part + 1) * 8]:
            copy.wait()
        hi, low = split2(rows_ref[part * 8:(part + 1) * 8].reshape(8 * XB, NR))
        modes = lax.dot_general(
            jnp.concatenate([q_ref[0], q_ref[0], q_ref[1]], axis=1), jnp.concatenate([hi, low, hi], axis=1),
            contract, preferred_element_type=jnp.float32)
        for m in range(MODES):
            for c in range(3):
                out_ref[pl.ds(m * TILES_IN + part * 3 + c, DEV, stride=MODES * TILES_IN), :] = (
                    modes[m * DEV:(m + 1) * DEV, c * 128:(c + 1) * 128])


def forward_third(density, q):
    return pl.pallas_call(
        forward_kernel,
        out_shape=pltpu.HBM((DEV * MODES * TILES_IN, 128), jnp.float32),
        in_specs=[pl.BlockSpec(memory_space=pltpu.HBM), pl.BlockSpec(memory_space=pltpu.HBM)],
        out_specs=pl.BlockSpec(memory_space=pltpu.VMEM),
        scratch_shapes=[pltpu.VMEM((YB, XB, NR), jnp.float32), pltpu.VMEM((2, NR, NR), jnp.bfloat16),
                        pltpu.SemaphoreType.DMA((YB + 1,))],
        compiler_params=pltpu.CompilerParams(vmem_limit_bytes=16 << 20),
        name="forward_third",
    )(in_hbm(density), in_hbm(table_pair(q.T)))


def plane_kernel(mode_ref, in_ref, ax_ref, ay_ref, by_ref, bx_ref, ey_ref, ex_ref, out_ref, x_ref, o_ref):
    lane = lax.broadcasted_iota(jnp.int32, (8, 128), 1)
    stride_in = MODES * TILES_IN
    stride_out = MODES * TILES_OUT
    second = [jnp.broadcast_to(ey_ref[i:i + 1, :], (128, 256)).T[:NR // 2, :1] for i in range(2)]
    def unpack(m):
        for y in range(YB):
            for h in range(2):
                even, odd = [None, None], [None, None]
                for p in range(PX // 2):
                    loaded = {}

                    def pair(c):
                        if c not in loaded:
                            near = in_ref[pl.ds((p * PY + h * 8) * stride_in + m * TILES_IN + c, 8, stride=stride_in), :]
                            far = in_ref[pl.ds(((p + PX // 2) * PY + h * 8) * stride_in + m * TILES_IN + c, 8,
                                               stride=stride_in), :]
                            loaded[c] = (near + far, near - far)
                        return loaded[c]

                    moved(lambda c: pair(c)[0], y * XB, p * XB, XB, lane, even)
                    moved(lambda c: pair(c)[1], y * XB, p * XB, XB, lane, odd)
                row = y * PY + h * 8
                for t, tile in enumerate(even + odd):
                    x_ref[m, row:row + 8, t * 128:(t + 1) * 128] = tile

    def transform(m):
        z = jnp.concatenate([right_product(x_ref[m, :, i * 256:(i + 1) * 256], ax_ref.at[i]) for i in range(2)], axis=1)
        z = z.reshape(YB, PY, 512)
        near = z[:, :8].reshape(YB * 8, 512)
        far = z[:, 8:].reshape(YB * 8, 512)
        halves = []
        for i, z in enumerate((near + far, near - far)):
            z = left_product(ay_ref.at[i], z)
            total = mode_ref[m] + second[i] + ex_ref[...]
            is_zero = total == 0.0
            z = jnp.where(is_zero, 0.0, z / jnp.where(is_zero, -1.0, total))
            halves.append(left_product(by_ref.at[i], z))
        z = jnp.concatenate([halves[0] + halves[1], halves[0] - halves[1]], axis=0)
        even, odd = (right_product(z[:, i * 256:(i + 1) * 256], bx_ref.at[i]) for i in range(2))
        o_ref[m, :, :256] = even + odd
        o_ref[m, :, 256:] = even - odd

    def pack(m):
        for p in range(PX):
            for h in range(2):
                out = [None] * TILES_OUT
                for y in range(YE):
                    row = h * YE * 8 + y * 8
                    moved(lambda t: o_ref[m, row:row + 8, t * 128:(t + 1) * 128], p * 64, y * XE, XE, lane, out)
                for t in range(TILES_OUT):
                    out_ref[pl.ds((p * PY + h * 8) * stride_out + m * TILES_OUT + t, 8, stride=stride_out), :] = out[t]

    unpack(0)
    transform(0)
    unpack(1)
    transform(1)
    pack(0)
    unpack(2)
    transform(2)
    pack(1)
    pack(2)


def solve_planes(own_eig, got, q, eig):
    k = np.rint(np.arcsin(np.sqrt(-eig / 4.0)) * NR / np.pi).astype(int)
    n = np.arange(NR // 2)
    order = (n % 8) * YB + n // 8
    wide = ((np.arange(YE)[:, None] - 2 + np.arange(8)[None, :] * YB) % NR).reshape(-1)
    half = NR // 2
    tables = [[], [], [], []]
    ey = np.zeros((2, 256))
    ex = np.full((1, 512), -1.0)
    for i in range(2):
        part = q[:, k % 2 == i]
        ey[i, :half] = eig[k % 2 == i]
        ex[0, i * 256:i * 256 + half] = eig[k % 2 == i]
        ax = np.zeros((half, 256))
        ax[:half, :half] = part[:half]
        bx = np.zeros((half, PX // 2, 64))
        for p in range(PX // 2):
            bx[:half, p, :XE] = part[(p * XB + np.arange(XE) - 1) % NR].T
        for bucket, table in zip(tables, (ax, np.pad(part[order].T, ((0, 0), (0, 256 - half))),
                                          np.pad(part[wide], ((0, 0), (0, 256 - half))), bx.reshape(half, 256))):
            bucket.append(table_pair(table))
    tables = [jnp.stack(bucket) for bucket in tables]
    vmem = pl.BlockSpec(memory_space=pltpu.VMEM)
    return pl.pallas_call(
        plane_kernel,
        out_shape=pltpu.HBM((DEV * MODES * TILES_OUT, 128), jnp.float32),
        in_specs=[pl.BlockSpec(memory_space=pltpu.SMEM)] + [vmem] * 7,
        out_specs=vmem,
        scratch_shapes=[pltpu.VMEM((MODES, NR, 512), jnp.float32), pltpu.VMEM((MODES, YE * PY, 512), jnp.float32)],
        compiler_params=pltpu.CompilerParams(vmem_limit_bytes=20 << 20),
        name="solve_planes",
    )(own_eig, in_vmem(got), *tables, jnp.asarray(ey, jnp.float32), jnp.asarray(ex, jnp.float32))


def stacked_parts(s_ref):
    his, lows = [], []
    for m in range(MODES):
        rows = jnp.concatenate(
            [s_ref[pl.ds(m * TILES_OUT + c, DEV, stride=MODES * TILES_OUT), :] for c in range(TILES_OUT)], axis=1)
        hi, low = split2(rows)
        his.append(hi)
        lows.append(low)
    return jnp.concatenate(his + lows + his, axis=0)


def columns_of(stacked, hi, low):
    right = jnp.concatenate([hi, hi, low], axis=0)
    return lax.dot_general(stacked, right, (((0,), (0,)), ((), ())), preferred_element_type=jnp.float32)


def cut_kernel(start_ref, s_ref, g_ref, out_ref, p_ref):
    cells = columns_of(stacked_parts(s_ref), *split2(g_ref[...]))
    for y in range(YE):
        p_ref[y, :XE, :] = cells[y * XE:(y + 1) * XE, :]
    lane = lax.broadcasted_iota(jnp.int32, (16, 128), 1)
    inside = lax.broadcasted_iota(jnp.int32, (16, 128), 0) < REG + 2
    for t in range(PY):
        acc = jnp.zeros((16, 128), jnp.float32)
        for b in range(12):
            first = pl.multiple_of(start_ref[t, 0], 8)
            tile = p_ref[start_ref[t, 1] + b, pl.ds(first, 16), (t // 8) * 128:(t // 8 + 1) * 128]
            shift = (b * 10 - (t % 8) * 16) % 128
            if shift:
                tile = pltpu.roll(tile, shift, 1)
            acc = jnp.where((lane >= b * 10) & (lane < b * 10 + 10) & inside, tile, acc)
        out_ref[t * 16:(t + 1) * 16, :] = acc


def cut_patches(spectrum, columns, starts):
    return pl.pallas_call(
        cut_kernel,
        out_shape=jax.ShapeDtypeStruct((PY * 16, 128), jnp.float32),
        in_specs=[pl.BlockSpec(memory_space=pltpu.SMEM),
                  pl.BlockSpec(memory_space=pltpu.VMEM),
                  pl.BlockSpec(memory_space=pltpu.VMEM)],
        out_specs=pl.BlockSpec(memory_space=pltpu.VMEM),
        scratch_shapes=[pltpu.VMEM((YE, 56, 256), jnp.float32)],
        compiler_params=pltpu.CompilerParams(vmem_limit_bytes=12 << 20),
        name="cut_patches",
    )(starts, spectrum, columns)


def block_kernel(s_ref, q_hbm, out_ref, q_ref, sem):
    copy = pltpu.make_async_copy(q_hbm, q_ref, sem)
    copy.start()
    stacked = stacked_parts(s_ref)
    copy.wait()
    cells = columns_of(stacked, q_ref[0], q_ref[1])
    for y in range(YB):
        first = (y + 2) * XE + 1
        out_ref[:, y, :] = cells[first:first + XB, :]


def block_of(spectrum, q):
    return pl.pallas_call(
        block_kernel,
        out_shape=jax.ShapeDtypeStruct((XB, YB, NR), jnp.float32),
        in_specs=[pl.BlockSpec(memory_space=pltpu.VMEM), pl.BlockSpec(memory_space=pltpu.HBM)],
        out_specs=pl.BlockSpec(memory_space=pltpu.VMEM),
        scratch_shapes=[pltpu.VMEM((2, NR, NR), jnp.bfloat16), pltpu.SemaphoreType.DMA],
        compiler_params=pltpu.CompilerParams(vmem_limit_bytes=14 << 20),
        name="block_of",
    )(spectrum, in_hbm(table_pair(q.T)))


def relax_kernel(flag_ref, patch_ref, rows_ref, cols_ref, dens_hbm, low_ref, high_ref, vel_hbm,
                 pot_hbm, out_hbm, grid_ref, v_ref, f_ref, dens_ref, vel_ref, beside_ref, in_sem, out_sem):
    step = pl.program_id(0)

    def arrivals(s):
        return (pltpu.make_async_copy(dens_hbm.at[s], dens_ref.at[s], in_sem.at[0, s]),
                pltpu.make_async_copy(vel_hbm.at[:, s], vel_ref.at[:, s], in_sem.at[1, s]))

    def departures(s):
        return (pltpu.make_async_copy(dens_ref.at[s], pot_hbm.at[s], out_sem.at[0, s]),
                pltpu.make_async_copy(vel_ref.at[:, s], out_hbm.at[:, s], out_sem.at[1, s]))

    @pl.when(step == 0)
    def _():
        for s in range(PY):
            for copy in arrivals(s):
                copy.start()

    @pl.when(step == 0)
    def _():
        source = lax.broadcasted_iota(jnp.int32, (512, 256), 0) % 256
        target = lax.broadcasted_iota(jnp.int32, (512, 256), 1)
        apart = jnp.abs(source - target)
        near = (apart == CELLS) | ((apart == 1) & (source // CELLS == target // CELLS))
        beside_ref[...] = jnp.where(near, 1.0, 0.0).astype(jnp.bfloat16)
        rows = rows_ref[...]
        ordered = jnp.concatenate(
            [patch_ref[pl.ds(pl.multiple_of(flag_ref[j, 7] * 16, 16), 16), :] for j in range(PY)], axis=0)
        expanded = jnp.zeros((640, 128), jnp.float32)
        for part in split3(ordered):
            expanded += dot(rows, part)
        pair = jnp.concatenate(split2(expanded), axis=1)
        for n in range(0, 2 * LANES, 256):
            table = cols_ref[:, n:n + 256]
            grid_ref[:, n:n + 256] = dot(pair, jnp.concatenate([table, table], axis=0))

    tiles = LANES // 128
    lane = lax.broadcasted_iota(jnp.int32, (8, 128), 1)
    third_first = lane % CELLS == 0
    third_last = lane % CELLS == CELLS - 1
    second_first = lane < CELLS
    second_last = lane >= 128 - CELLS
    zero = jnp.zeros((8, 128), jnp.float32)
    slot_of = [step * GROUP + g for g in range(GROUP)]
    bases = [pl.multiple_of(s * 40, 8) for s in slot_of]
    flag = lambda g, i: jnp.broadcast_to(flag_ref[slot_of[g], i + 2], (8, 128)) > 0
    use_low, use_high, same_low, same_high, live = ([flag(g, i) for g in range(GROUP)] for i in range(5))

    def start(g, t, r):
        return grid_ref[pl.ds(bases[g] + r * 8, 8), t * 128:(t + 1) * 128]

    def edge(g, t, r):
        return grid_ref[pl.ds(bases[g] + r * 8, 8), LANES + t * 128:LANES + (t + 1) * 128]

    def row_of(buffer, g, t, r):
        return ((buffer * GROUP + g) * tiles + t) * ROWS + 8 + r * 8

    def value(buffer, g, t, r):
        row = row_of(buffer, g, t, r)
        return v_ref[row:row + 8, :]

    def first_neighbours(buffer, g, t, r):
        row = row_of(buffer, g, t, r)
        return v_ref[row - 1:row + 7, :], v_ref[row + 1:row + 9, :]

    def prepare(g):
        s = slot_of[g]
        for copy in arrivals(s):
            copy.wait()
        for t in range(tiles):
            faces = grid_ref[pl.ds(bases[g] + 32, 8), t * 128:(t + 1) * 128]
            for buffer in range(2):
                row = row_of(buffer, g, t, 0)
                v_ref[row - 1:row, :] = faces[0:1]
                v_ref[row + CELLS:row + CELLS + 1, :] = faces[1:2]
            for r in range(4):
                rows = slice(r * 8, r * 8 + 8)
                if t == 0:
                    rho = low_ref[s, rows, :]
                elif t == tiles - 1:
                    rho = high_ref[s, rows, :]
                else:
                    rho = dens_ref[s, rows, (t - 1) * 128:t * 128]
                fixed = edge(g, t, r) - rho * (1.0 / (REF * REF))
                if t == 0:
                    fixed -= jnp.where(second_first, pltpu.roll(start(g, tiles - 1, r), CELLS, 1), zero)
                if t == tiles - 1:
                    fixed -= jnp.where(second_last, pltpu.roll(start(g, 0, r), 128 - CELLS, 1), zero)
                f_ref[g, t, r] = fixed
                row = row_of(0, g, t, r)
                v_ref[row:row + 8, :] = start(g, t, r)

    pairs = [(tiles - 1, 0)] + [(t, t + 1) for t in range(1, tiles - 1, 2)]
    beside = beside_ref[...]

    def around_of(buffer, members):
        stacked = jnp.concatenate([
            jnp.concatenate([v_ref[row_of(buffer, g, t, 0):row_of(buffer, g, t, 4), :] for t in pair], axis=1)
            for g in members for pair in pairs
        ], axis=0)
        return dot(jnp.concatenate(split2(stacked), axis=1), beside)

    def update(buffer, members, around):
        for m, g in enumerate(members):
            for p, pair in enumerate(pairs):
                for side, t in enumerate(pair):
                    for r in range(4):
                        here = value(buffer, g, t, r)
                        if side == 0:
                            other = pltpu.roll(value(buffer, g, t - 1, r), CELLS, 1)
                            if t == tiles - 1:
                                other = jnp.where(same_high[g], other, pltpu.roll(start(g, t - 1, r), CELLS, 1))
                            other = jnp.where(second_first, other, zero)
                        else:
                            other = pltpu.roll(value(buffer, g, t + 1, r), 128 - CELLS, 1)
                            if t == 0:
                                other = jnp.where(same_low[g], other, pltpu.roll(start(g, t + 1, r), 128 - CELLS, 1))
                            other = jnp.where(second_last, other, zero)
                        before, after = first_neighbours(buffer, g, t, r)
                        row = (m * len(pairs) + p) * CELLS + r * 8
                        total = (here + f_ref[g, t, r]) + (before + after) + (
                            around[row:row + 8, side * 128:(side + 1) * 128] + other)
                        new = total * (1.0 - RELAX)
                        if t == 0:
                            new = jnp.where(use_low[g], new, here)
                        if t == tiles - 1:
                            new = jnp.where(use_high[g], new, here)
                        row = row_of(1 - buffer, g, t, r)
                        v_ref[row:row + 8, :] = new

    def kick(buffer, g):
        s = slot_of[g]
        for r in range(4):
            values = [value(buffer, g, t, r) for t in range(tiles)]
            up = [pltpu.roll(here, CELLS, 1) for here in values]
            down = [pltpu.roll(here, 128 - CELLS, 1) for here in values]
            for t in range(1, tiles - 1):
                here = values[t]
                rows = slice(r * 8, r * 8 + 8)
                cols = slice((t - 1) * 128, t * 128)
                dens_ref[s, rows, cols] = jnp.where(live[g], here, 0.0)
                wall = edge(g, t, r)
                ends = (
                    first_neighbours(buffer, g, t, r),
                    (jnp.where(second_first, up[t - 1], up[t]), jnp.where(second_last, down[t + 1], down[t])),
                    (jnp.where(third_first, wall, pltpu.roll(here, 1, 1)),
                     jnp.where(third_last, wall, pltpu.roll(here, 127, 1))),
                )
                for q, (before, after) in enumerate(ends):
                    kicked = vel_ref[q, s, rows, cols] - (after - before) * (REF / 2.0)
                    vel_ref[q, s, rows, cols] = jnp.where(live[g], kicked, 0.0)
        for copy in departures(s):
            copy.start()

    halves = [range(0, GROUP // 2), range(GROUP // 2, GROUP)]
    for g in range(GROUP):
        prepare(g)
    for sweep in range(SWEEPS):
        buffer = sweep % 2
        arounds = [around_of(buffer, members) for members in halves]
        for members, around in zip(halves, arounds):
            update(buffer, members, around)
    for g in range(GROUP):
        kick(SWEEPS % 2, g)

    @pl.when(step == pl.num_programs(0) - 1)
    def _():
        for s in range(PY):
            for copy in departures(s):
                copy.wait()


def relax(flags, patch, density, low, high, velocity):
    slots = density.shape[0]
    rows, cols = interpolation_tables()
    block_rows = jnp.asarray(np.kron(np.eye(slots), rows), jnp.bfloat16)
    table = jnp.asarray(cols, jnp.bfloat16)
    whole = lambda shape: pl.BlockSpec(shape, lambda s, f: (0,) * len(shape), pipeline_mode=pl.Buffered(1))
    return pl.pallas_call(
        relax_kernel,
        grid_spec=pltpu.PrefetchScalarGridSpec(
            num_scalar_prefetch=1,
            grid=(slots // GROUP,),
            in_specs=[
                whole((slots * 16, 128)),
                whole((slots * 40, slots * 16)),
                whole((128, 2 * LANES)),
                pl.BlockSpec(memory_space=pltpu.HBM),
                pl.BlockSpec(memory_space=pltpu.VMEM),
                pl.BlockSpec(memory_space=pltpu.VMEM),
                pl.BlockSpec(memory_space=pltpu.HBM),
            ],
            out_specs=[pl.BlockSpec(memory_space=pltpu.HBM), pl.BlockSpec(memory_space=pltpu.HBM)],
            scratch_shapes=[
                pltpu.VMEM((slots * 40, 2 * LANES), jnp.float32),
                pltpu.VMEM((2 * GROUP * (LANES // 128) * ROWS, 128), jnp.float32),
                pltpu.VMEM((GROUP, LANES // 128, 4, 8, 128), jnp.float32),
                pltpu.VMEM((slots, CELLS, CELLS * CELLS), jnp.float32),
                pltpu.VMEM((3, slots, CELLS, CELLS * CELLS), jnp.float32),
                pltpu.VMEM((512, 256), jnp.bfloat16),
                pltpu.SemaphoreType.DMA((2, slots)),
                pltpu.SemaphoreType.DMA((2, slots)),
            ],
        ),
        out_shape=[
            pltpu.HBM((slots, CELLS, CELLS * CELLS), jnp.float32),
            pltpu.HBM((3, slots, CELLS, CELLS * CELLS), jnp.float32),
        ],
        compiler_params=pltpu.CompilerParams(vmem_limit_bytes=34 << 20),
        name="relax_and_kick",
    )(flags, patch, block_rows, table, in_hbm(density), low, high, in_hbm(velocity))


def local(root_density, subgrid_density, velocity, slot_anchor, slot_count, neighbour):
    place_first = lax.axis_index("px")
    place_second = lax.axis_index("py")
    device = place_first * PY + place_second
    slots = subgrid_density.shape[0]
    q, eig = fourier_basis()
    basis = jnp.asarray(q, jnp.float32)
    eigen = jnp.asarray(eig, jnp.float32)
    low = from_behind(subgrid_density[:, :, -EDGE * CELLS:], "py", 1)
    high = from_behind(subgrid_density[:, :, :EDGE * CELLS], "py", -1)

    packed = forward_third(root_density, q)
    packed = packed.reshape(DEV, 1, MODES * YB * XB)
    got = lax.all_to_all(packed, ("px", "py"), 0, 0, tiled=True).reshape(-1, 128)
    own_eig = eigen[jnp.arange(MODES) * DEV + device]
    solved = solve_planes(own_eig, got, q, eig).reshape(DEV, 1, MODES * PLANE)
    back = lax.all_to_all(solved, ("px", "py"), 0, 0, tiled=True).reshape(-1, 128)

    targets = jnp.arange(PY, dtype=jnp.int32)
    wanted = (place_first * PY + targets) * slots + (place_second - targets) % PY
    anchors = slot_anchor[:, wanted]
    third = (anchors[2][:, None] - 1 + jnp.arange(16, dtype=jnp.int32)[None, :]) % NR
    columns = basis[third.reshape(-1)].T
    start_first = jnp.clip(anchors[0] - place_first * XB, 0, XB - REG)
    start_second = jnp.clip(anchors[1] - place_second * YB, 0, YB - REG)
    positions = jnp.arange(slots, dtype=jnp.int32)
    first_slot = device * slots
    padded = jnp.pad(neighbour, ((0, 0), (slots, slots)), constant_values=-1)
    nearby = lax.dynamic_slice_in_dim(neighbour, first_slot, slots, 1)
    below = lax.dynamic_slice_in_dim(padded, first_slot, slots, 1)
    above = lax.dynamic_slice_in_dim(padded, first_slot + 2 * slots, slots, 1)
    flags = jnp.stack([
        start_first, start_second,
        nearby[0] >= 0, nearby[1] >= 0, below[1] >= 0, above[0] >= 0,
        positions < slot_count[device], (place_second + positions) % PY,
    ], axis=1).astype(jnp.int32)
    sending = cut_patches(back, columns, flags)
    arrived = lax.all_to_all(sending, "py", 0, 0, tiled=True)

    coarse_potential = block_of(back, q)

    subgrid_potential, kicked = relax(flags, arrived, subgrid_density, low, high, velocity)
    return coarse_potential, subgrid_potential, kicked


def solution(mesh):
    return jax.shard_map(
        local,
        mesh=mesh,
        in_specs=(
            P("px", "py", None),
            P(("px", "py"), None, None),
            P(None, ("px", "py"), None, None),
            P(),
            P(),
            P(),
        ),
        out_specs=(
            P("px", "py", None),
            P(("px", "py"), None, None),
            P(None, ("px", "py"), None, None),
        ),
        check_vma=False,
    )
```
